128 devices in a mesh: row: 8 (over z, x_lo), col: 16 (over x_hi, y, core).
Axes of the slice: x: 4 (x_hi: 2, x_lo: 2; x = x_hi * 2 + x_lo), y: 4, z: 4, core: 2. Of those that a mesh axis runs over, the one named last changes fastest.
Arguments:
- tile_values: bfloat16 [8, 16, 256, 128, 128], P('row', 'col'), may hold values from -0.09375 to 0.09375
- tile_rows: int32 [8, 16, 256], P('row', 'col'), may hold values from 0 to 127
- tile_cols: int32 [8, 16, 256], P('row', 'col'), may hold values from 0 to 255
- increments: float32 [16, 128, 4096], P('row', None, 'col'), may hold values from 0 to 0.1
- dual_vars: float32 [16, 131072], P(None, 'row'), may hold values from 0 to 1
- flight_cost: float32 [128, 4096], P(None, 'col'), may hold values from -0.5 to 0.5
- win_start: int32 [4096], P('col'), may hold values from 0 to 63
- win_len: int32 [4096], P('col'), may hold values from 32 to 64
- capacity: int32 [16, 131072], P(None, 'row'), may hold values from 0 to 3
Outputs:
- primal: float32 [16, 128, 4096], P('row', None, 'col')
- duals_out: float32 [16, 131072], P(None, 'row')
The draws below stay inside these ranges and needn't reach their ends.
Inputs may be any that keep to these rules, and one draw needn't show every extreme that they name: `tile_rows`: a block position may occur more than once in a device's list; such blocks add.
All inputs are finite; a program needn't handle non-finite values.
Results may differ from the reference program's by a relative error of at most 0.0056.
Values may be sent and summed in bfloat16 or wider, within the bound.
A program may use at most 64 MiB of HBM per device.

```python
import math
import jax
import jax.numpy as jnp
from jax import lax

TILE = 128
SCEN = 16
WINDOW = 128
ITERS = 2
ROW_TILES = 128
TILES_DEV = 256
FLIGHTS = 4096
COL_TILES = 256
ROWS = 131072
N_ROW = 8
N_COL = 16


def set_ends(array, key, least, largest):
    longest = array.shape.index(max(array.shape))
    spots = []
    for shift in (0, 1):
        where = [jax.random.randint(jax.random.fold_in(key, axis), (), 0, length) for axis, length in enumerate(array.shape)]
        where[longest] = (where[longest] + shift) % array.shape[longest]
        spots.append(tuple(where))
    return array.at[spots[0]].set(least).at[spots[1]].set(largest)


def levels(own_key, dims, shards, low, high):
    factor_of, own = 1.0, jax.random.fold_in(own_key, 6)
    for position, blocks in shards:
        steps = jnp.exp(jax.random.uniform(jax.random.fold_in(own, position), (blocks,), jnp.float32, low / len(shards), high / len(shards)))
        factor_of = factor_of * jnp.repeat(steps, dims[position] // blocks).reshape([-1 if axis == position else 1 for axis in range(len(dims))])
    return factor_of


def bell_draw(key, extent, spread, limit, pieces=(), dtype=jnp.bfloat16):
    array = spread * jax.random.normal(key, extent, jnp.float32)
    if pieces:
        array = array * levels(key, extent, pieces, -0.22, 0.18)
    return jnp.clip(array, -limit, limit).astype(dtype)


def setup_inputs(seed: int = 0) -> dict:
    key_list = jax.random.split(jax.random.key(seed), 10)
    return {
        "tile_values": bell_draw(key_list[0], (N_ROW, N_COL, TILES_DEV, TILE, TILE), (TILE * N_COL * TILES_DEV // ROW_TILES) ** -0.5, 0.09375, ((0, 8), (1, 16))),
        "tile_rows": set_ends(jax.random.randint(key_list[1], (N_ROW, N_COL, TILES_DEV), 0, ROW_TILES), jax.random.fold_in(key_list[1], 1), 0, ROW_TILES - 1).astype(jnp.int32),
        "tile_cols": set_ends(jax.random.randint(key_list[2], (N_ROW, N_COL, TILES_DEV), 0, COL_TILES), jax.random.fold_in(key_list[2], 1), 0, COL_TILES - 1).astype(jnp.int32),
        "increments": jnp.clip(0.1 * jax.random.uniform(key_list[3], (SCEN, WINDOW, FLIGHTS), jnp.float32) ** levels(key_list[3], (SCEN, WINDOW, FLIGHTS), ((0, 8), (2, 16)), -0.2, 0.2), 0.0, 0.1),
        "dual_vars": jnp.clip(1.0 * jax.random.uniform(key_list[4], (SCEN, ROWS), jnp.float32) ** levels(key_list[4], (SCEN, ROWS), ((1, 8),), -0.2, 0.2), 0.0, 1.0),
        "flight_cost": jnp.clip(jax.random.uniform(key_list[5], (WINDOW, FLIGHTS), jnp.float32, -0.5, 0.5) * levels(key_list[5], (WINDOW, FLIGHTS), ((1, 16),), -0.4, 0.0), -0.5, 0.5),
        "win_start": set_ends(jax.random.randint(key_list[6], (FLIGHTS,), 0, WINDOW // 2), jax.random.fold_in(key_list[6], 1), 0, (WINDOW // 2) - 1).astype(jnp.int32),
        "win_len": set_ends(jax.random.randint(key_list[7], (FLIGHTS,), WINDOW // 4, WINDOW // 2 + 1), jax.random.fold_in(key_list[7], 1), WINDOW // 4, (WINDOW // 2 + 1) - 1).astype(jnp.int32),
        "capacity": set_ends(jax.random.randint(key_list[8], (SCEN, ROWS), 0, 4), jax.random.fold_in(key_list[8], 1), 0, 3).astype(jnp.int32),
    }


SIGMA_STEP = 0.2

def running_total(values):
    length = values.shape[1]
    row_iota = lax.broadcasted_iota(jnp.int32, (length, length), 0)
    col_iota = lax.broadcasted_iota(jnp.int32, (length, length), 1)
    triangle = (row_iota >= col_iota).astype(jnp.float32)
    return jnp.einsum('kj,sjf->skf', triangle, values, precision=lax.Precision.HIGHEST)

def trailing_total(values):
    length = values.shape[1]
    row_iota = lax.broadcasted_iota(jnp.int32, (length, length), 0)
    col_iota = lax.broadcasted_iota(jnp.int32, (length, length), 1)
    triangle = (row_iota >= col_iota).astype(jnp.float32)
    return jnp.einsum('jk,sjf->skf', triangle, values, precision=lax.Precision.HIGHEST)

def forward_blocks(tile_values, tile_rows, tile_cols, probe_blocks):
    row_iota = jnp.arange(ROW_TILES).astype(jnp.int32)

    def one_group(group):

        def add_block(carried, column):
            picked = jnp.take(probe_blocks[:, column], tile_cols[group, column], axis=0 + 1).astype(jnp.float32)
            products = jnp.einsum('nij,snj->sni', tile_values[group, column].astype(jnp.float32), picked)
            hot_rows = (tile_rows[group, column][None, :] == row_iota[:, None]).astype(jnp.float32)
            return (carried + jnp.einsum('rn,sni->sri', hot_rows, products), None)
        start_sum = jnp.zeros((SCEN, ROW_TILES, TILE), jnp.float32)
        summed, _ = lax.scan(add_block, start_sum, jnp.arange(N_COL).astype(jnp.int32))
        return summed
    stacked = lax.map(one_group, jnp.arange(N_ROW).astype(jnp.int32))
    return jnp.transpose(stacked, (1, 0, 2, 3))

def backward_blocks(tile_values, tile_rows, tile_cols, dual_blocks):
    col_iota = jnp.arange(COL_TILES).astype(jnp.int32)

    def one_group(column):

        def add_block(carried, group):
            picked = jnp.take(dual_blocks[:, group], tile_rows[group, column], axis=1).astype(jnp.float32)
            products = jnp.einsum('nij,sni->snj', tile_values[group, column].astype(jnp.float32), picked)
            hot_cols = (tile_cols[group, column][None, :] == col_iota[:, None]).astype(jnp.float32)
            return (carried + jnp.einsum('cn,snj->scj', hot_cols, products), None)
        start_sum = jnp.zeros((SCEN, COL_TILES, TILE), jnp.float32)
        summed, _ = lax.scan(add_block, start_sum, jnp.arange(N_ROW).astype(jnp.int32))
        return summed
    stacked = lax.map(one_group, jnp.arange(N_COL).astype(jnp.int32))
    return jnp.transpose(stacked, (1, 0, 2, 3))

def reference(tile_values, tile_rows, tile_cols, increments, dual_vars, flight_cost, win_start, win_len, capacity):
    tau_step = 0.6 / math.sqrt(WINDOW)
    minutes = lax.broadcasted_iota(jnp.int32, (WINDOW, FLIGHTS), 0)
    upper_bound = ((minutes >= win_start[None, :]) & (minutes < (win_start + win_len)[None, :])).astype(jnp.float32)
    capacity_f = capacity.astype(jnp.float32)
    primal = increments
    cumulative = running_total(primal)
    for sweep_index in range(ITERS):
        dual_blocks = dual_vars.astype(jnp.bfloat16).reshape(SCEN, N_ROW, ROW_TILES, TILE)
        slope_all = backward_blocks(tile_values, tile_rows, tile_cols, dual_blocks).reshape(SCEN, WINDOW, FLIGHTS) + flight_cost[None]
        gradient = trailing_total(slope_all)
        primal = jnp.clip(primal - tau_step * gradient, 0.0, upper_bound[None])
        fresh_sum = running_total(primal)
        probe_vec = (2.0 * fresh_sum - cumulative).astype(jnp.bfloat16)
        image_rows = forward_blocks(tile_values, tile_rows, tile_cols, probe_vec.reshape(SCEN, N_COL, COL_TILES, TILE)).reshape(SCEN, ROWS)
        dual_vars = jnp.maximum(dual_vars + SIGMA_STEP * (image_rows - capacity_f), 0.0)
        cumulative = fresh_sum
    return (primal, dual_vars)
```

```python
import functools
import math

import jax
import jax.numpy as jnp
from jax import lax
from jax.experimental import pallas as pl
from jax.experimental.pallas import tpu as pltpu
from jax.sharding import PartitionSpec as P

ITERS = 2
SIGMA_STEP = 0.2
MESH = pl.DeviceIdType.MESH
F32, BF16 = jnp.float32, jnp.bfloat16
LOAD_CHUNKS = 8


def kernel(
    dims,
    values_hbm,
    row_of,
    col_of,
    row_vec,
    col_vec,
    inc_ref,
    dual_ref,
    cost_ref,
    start_ref,
    len_ref,
    cap_ref,
    primal_ref,
    duals_ref,
    blocks,
    hot_cols,
    hot_rows,
    products,
    by_tile,
    slope_send,
    slope_recv,
    slope,
    cumulative,
    probe_send,
    probe_recv,
    image_send,
    image_recv,
    own_dual,
    own_cap,
    own_send,
    duals_recv,
    load_sem,
    local_sem,
    send_sem,
    slope_sem,
    probe_sem,
    row_send_sem,
    image_sem,
    dual_sem,
):
    n_row, n_col, scenarios, scen_local, window, tiles, row_tiles, col_tiles = dims
    devices = n_row * n_col
    block_rows = 16
    per_load = tiles // LOAD_CHUNKS
    picked = by_tile.reshape(by_tile.shape[0] * scenarios, by_tile.shape[2])
    tau_step = 0.6 / math.sqrt(window)
    me_r, me_c = lax.axis_index("row"), lax.axis_index("col")
    me = me_r * n_col + me_c

    def load(chunk):
        span = pl.ds(chunk * per_load, per_load)
        return pltpu.make_async_copy(
            values_hbm.at[span], blocks.at[span], load_sem.at[chunk]
        )

    for chunk in range(LOAD_CHUNKS):
        load(chunk).start()

    def peer_of(step):
        peer = lax.rem(me + step, devices)
        return peer, peer // n_col, lax.rem(peer, n_col)

    barrier = pltpu.get_barrier_semaphore()

    @pl.loop(1, devices)
    def _(step):
        _, peer_r, peer_c = peer_of(step)
        pl.semaphore_signal(barrier, inc=1, device_id=(peer_r, peer_c), device_id_type=MESH)

    def slope_copy(peer_r, peer_c):
        return pltpu.make_async_remote_copy(
            src_ref=slope_send.at[
                pl.ds(peer_r * scen_local, scen_local),
                pl.ds(pl.multiple_of(peer_c * block_rows, block_rows), block_rows),
            ],
            dst_ref=slope_recv.at[me],
            send_sem=send_sem.at[peer_r * n_col + peer_c],
            recv_sem=slope_sem.at[me],
            device_id=(peer_r, peer_c),
            device_id_type=MESH,
        )

    def slope_arrival(peer, peer_r, peer_c):
        return pltpu.make_async_remote_copy(
            src_ref=slope_recv.at[peer],
            dst_ref=slope_recv.at[peer],
            send_sem=send_sem.at[peer],
            recv_sem=slope_sem.at[peer],
            device_id=(peer_r, peer_c),
            device_id_type=MESH,
        )

    def probe_place(r, c):
        return probe_recv.at[
            pl.ds(r * scen_local, scen_local),
            pl.ds(pl.multiple_of(c * block_rows, block_rows), block_rows),
        ]

    def probe_copy(peer_r, peer_c):
        return pltpu.make_async_remote_copy(
            src_ref=probe_send.at[peer_c],
            dst_ref=probe_place(me_r, me_c),
            send_sem=send_sem.at[peer_r * n_col + peer_c],
            recv_sem=probe_sem.at[me],
            device_id=(peer_r, peer_c),
            device_id_type=MESH,
        )

    def probe_arrival(peer, peer_r, peer_c):
        return pltpu.make_async_remote_copy(
            src_ref=probe_place(peer_r, peer_c),
            dst_ref=probe_place(peer_r, peer_c),
            send_sem=send_sem.at[peer],
            recv_sem=probe_sem.at[peer],
            device_id=(peer_r, peer_c),
            device_id_type=MESH,
        )

    def image_copy(peer_c):
        return pltpu.make_async_remote_copy(
            src_ref=image_send.at[peer_c],
            dst_ref=image_recv.at[me_c],
            send_sem=row_send_sem.at[peer_c],
            recv_sem=image_sem.at[me_c],
            device_id=(me_r, peer_c),
            device_id_type=MESH,
        )

    def image_arrival(peer_c):
        return pltpu.make_async_remote_copy(
            src_ref=image_recv.at[peer_c],
            dst_ref=image_recv.at[peer_c],
            send_sem=row_send_sem.at[peer_c],
            recv_sem=image_sem.at[peer_c],
            device_id=(me_r, peer_c),
            device_id_type=MESH,
        )

    def dual_copy(peer_c):
        return pltpu.make_async_remote_copy(
            src_ref=own_send,
            dst_ref=duals_recv.at[me_c],
            send_sem=row_send_sem.at[peer_c],
            recv_sem=dual_sem.at[me_c],
            device_id=(me_r, peer_c),
            device_id_type=MESH,
        )

    def dual_arrival(peer_c):
        return pltpu.make_async_remote_copy(
            src_ref=duals_recv.at[peer_c],
            dst_ref=duals_recv.at[peer_c],
            send_sem=row_send_sem.at[peer_c],
            recv_sem=dual_sem.at[peer_c],
            device_id=(me_r, peer_c),
            device_id_type=MESH,
        )

    hot_cols[...] = (
        col_vec[...] == lax.broadcasted_iota(jnp.int32, (col_tiles, tiles), 0)
    ).astype(F32).astype(BF16)
    hot_rows[...] = (
        row_vec[...] == lax.broadcasted_iota(jnp.int32, (row_tiles, tiles), 0)
    ).astype(F32).astype(BF16)

    @pl.loop(0, row_tiles)
    def _(tile):
        lanes = pl.ds(pl.multiple_of(tile * 128, 128), 128)
        rows = pl.ds(pl.multiple_of(tile * scenarios, scenarios), scenarios)
        products[rows, :] = cap_ref[:, lanes].astype(F32)
        picked[rows, :] = dual_ref[:, lanes]

    own_cap[...] = products[pl.ds(me_c, row_tiles, stride=scenarios), :]
    own_dual[...] = picked[pl.ds(me_c, row_tiles, stride=scenarios), :]

    row_iota = lax.broadcasted_iota(jnp.int32, (window, window), 0)
    col_iota = lax.broadcasted_iota(jnp.int32, (window, window), 1)
    running = (row_iota >= col_iota).astype(F32)
    trailing = (row_iota <= col_iota).astype(F32)
    flights = inc_ref.shape[2]

    def total(triangle, values):
        return jnp.dot(
            triangle, values, precision=lax.Precision.HIGHEST, preferred_element_type=F32
        )

    for scen in range(scen_local):
        primal_ref[scen] = inc_ref[scen]
        cumulative[scen] = total(running, inc_ref[scen])
    minutes = lax.broadcasted_iota(jnp.int32, (window, flights), 0)
    upper = (
        (minutes >= start_ref[...]) & (minutes < start_ref[...] + len_ref[...])
    ).astype(F32)

    for sweep in range(ITERS):
        for chunk in range(LOAD_CHUNKS):
            if sweep == 0:
                load(chunk).wait()

            @pl.loop(0, per_load // 8)
            def _(group):
                for k in range(8):
                    n = chunk * per_load + group * 8 + k
                    products[pl.ds(pl.multiple_of(n * scenarios, scenarios), scenarios), :] = (
                        jnp.dot(
                            by_tile[row_of[n]].astype(BF16),
                            blocks[n],
                            preferred_element_type=F32,
                        )
                    )

        if sweep == 0:
            pl.semaphore_wait(barrier, devices - 1)

        for group in range(n_row):
            for scen in range(group * scen_local, (group + 1) * scen_local):
                taken = products[pl.ds(scen, tiles, stride=scenarios), :].astype(BF16)
                slope_send[scen] = jnp.dot(
                    hot_cols[...], taken, preferred_element_type=F32
                ).astype(BF16)

        own = pltpu.make_async_copy(
            slope_send.at[
                pl.ds(me_r * scen_local, scen_local),
                pl.ds(pl.multiple_of(me_c * block_rows, block_rows), block_rows),
            ],
            slope_recv.at[me],
            local_sem.at[0],
        )
        own.start()

        @pl.loop(1, devices)
        def _(step):
            _, peer_r, peer_c = peer_of(step)
            slope_copy(peer_r, peer_c).start()

        own.wait()

        @pl.loop(1, devices)
        def _(step):
            peer, peer_r, peer_c = peer_of(devices - step)
            slope_arrival(peer, peer_r, peer_c).wait_recv()

        @pl.loop(0, n_col)
        def _(part):
            summed = slope_recv[part].astype(F32)
            for group in range(1, n_row):
                summed = summed + slope_recv[group * n_col + part].astype(F32)
            rows = pl.ds(pl.multiple_of(part * 8, 8), 8)
            for scen in range(scen_local):
                for half in range(flights // 128):
                    lanes = slice(half * 128, (half + 1) * 128)
                    slope[scen, rows, lanes] = (
                        summed[scen, half * 8 : (half + 1) * 8] + cost_ref[rows, lanes]
                    )

        @pl.loop(1, devices)
        def _(step):
            _, peer_r, peer_c = peer_of(step)
            slope_copy(peer_r, peer_c).wait_send()

        for scen in range(scen_local):
            gradient = total(trailing, slope[scen])
            fresh = jnp.clip(primal_ref[scen] - tau_step * gradient, 0.0, upper)
            primal_ref[scen] = fresh
            fresh_sum = total(running, fresh)
            probe = 2.0 * fresh_sum - cumulative[scen]
            cumulative[scen] = fresh_sum
            for part in range(n_col):
                probe_send[part, scen] = jnp.concatenate(
                    [
                        probe[part * 8 : (part + 1) * 8, half * 128 : (half + 1) * 128]
                        for half in range(flights // 128)
                    ],
                    axis=0,
                ).astype(BF16)

        own = pltpu.make_async_copy(
            probe_send.at[me_c], probe_place(me_r, me_c), local_sem.at[0]
        )
        own.start()

        @pl.loop(1, devices)
        def _(step):
            _, peer_r, peer_c = peer_of(step)
            probe_copy(peer_r, peer_c).start()

        own.wait()

        @pl.loop(1, devices)
        def _(step):
            peer, peer_r, peer_c = peer_of(devices - step)
            probe_arrival(peer, peer_r, peer_c).wait_recv()

        for scen in range(scenarios):
            picked[pl.ds(scen, col_tiles, stride=scenarios), :] = probe_recv[scen].astype(F32)

        @pl.loop(1, devices)
        def _(step):
            _, peer_r, peer_c = peer_of(step)
            probe_copy(peer_r, peer_c).wait_send()

        @pl.loop(0, tiles // 8)
        def _(group):
            for k in range(8):
                n = group * 8 + k
                products[pl.ds(pl.multiple_of(n * scenarios, scenarios), scenarios), :] = (
                    lax.dot_general(
                        by_tile[col_of[n]].astype(BF16),
                        blocks[n],
                        (((1,), (1,)), ((), ())),
                        preferred_element_type=F32,
                    )
                )

        for scen in range(scenarios):
            taken = products[pl.ds(scen, tiles, stride=scenarios), :].astype(BF16)
            image_send[scen] = jnp.dot(
                hot_rows[...], taken, preferred_element_type=F32
            ).astype(BF16)

        own = pltpu.make_async_copy(
            image_send.at[me_c], image_recv.at[me_c], local_sem.at[0]
        )
        own.start()

        @pl.loop(1, n_col)
        def _(step):
            image_copy(lax.rem(me_c + step, n_col)).start()

        own.wait()

        @pl.loop(1, n_col)
        def _(step):
            image_arrival(lax.rem(me_c + n_col - step, n_col)).wait_recv()

        image = image_recv[0].astype(F32)
        for part in range(1, n_col):
            image = image + image_recv[part].astype(F32)
        updated = jnp.maximum(own_dual[...] + SIGMA_STEP * (image - own_cap[...]), 0.0)
        own_dual[...] = updated
        own_send[...] = updated.astype(BF16)

        @pl.loop(1, n_col)
        def _(step):
            image_copy(lax.rem(me_c + step, n_col)).wait_send()

        own = pltpu.make_async_copy(own_send, duals_recv.at[me_c], local_sem.at[0])
        own.start()

        @pl.loop(1, n_col)
        def _(step):
            dual_copy(lax.rem(me_c + step, n_col)).start()

        own.wait()

        @pl.loop(1, n_col)
        def _(step):
            dual_arrival(lax.rem(me_c + n_col - step, n_col)).wait_recv()

        for scen in range(scenarios):
            picked[pl.ds(scen, row_tiles, stride=scenarios), :] = duals_recv[scen].astype(F32)

        @pl.loop(1, n_col)
        def _(step):
            dual_copy(lax.rem(me_c + step, n_col)).wait_send()

    @pl.loop(0, row_tiles)
    def _(tile):
        duals_ref[:, pl.ds(pl.multiple_of(tile * 128, 128), 128)] = picked[
            pl.ds(pl.multiple_of(tile * scenarios, scenarios), scenarios), :
        ]


def per_device(
    tile_values,
    tile_rows,
    tile_cols,
    increments,
    dual_vars,
    flight_cost,
    win_start,
    win_len,
    capacity,
):
    n_row, n_col = lax.axis_size("row"), lax.axis_size("col")
    tiles, side = tile_values.shape[2], tile_values.shape[3]
    scen_local, window, flight_local = increments.shape
    scenarios, row_length = dual_vars.shape
    row_tiles = row_length // side
    time_block = window // n_col
    flight_tiles = flight_local * n_col // side
    col_tiles = time_block * flight_tiles
    assert scenarios == n_col and time_block == 8 and flight_local == 256
    devices = n_row * n_col
    row_index = tile_rows.reshape(tiles)
    col_index = tile_cols.reshape(tiles)
    col_place = lax.rem(col_index, flight_tiles) * time_block + col_index // flight_tiles
    dims = (n_row, n_col, scenarios, scen_local, window, tiles, row_tiles, col_tiles)
    vmem = pl.BlockSpec(memory_space=pltpu.VMEM)
    smem = pl.BlockSpec(memory_space=pltpu.SMEM)
    dma = pltpu.SemaphoreType.DMA
    return pl.pallas_call(
        functools.partial(kernel, dims),
        out_shape=(
            jax.ShapeDtypeStruct(increments.shape, F32),
            jax.ShapeDtypeStruct(dual_vars.shape, F32),
        ),
        in_specs=[pl.BlockSpec(memory_space=pl.ANY), smem, smem] + [vmem] * 8,
        out_specs=(vmem, vmem),
        scratch_shapes=[
            pltpu.VMEM((tiles, side, side), BF16),
            pltpu.VMEM((col_tiles, tiles), BF16),
            pltpu.VMEM((row_tiles, tiles), BF16),
            pltpu.VMEM((max(tiles, row_tiles) * scenarios, side), F32),
            pltpu.VMEM((max(col_tiles, row_tiles), scenarios, side), F32),
            pltpu.VMEM((scenarios, col_tiles, side), BF16),
            pltpu.VMEM((devices, scen_local, 16, side), BF16),
            pltpu.VMEM((scen_local, window, flight_local), F32),
            pltpu.VMEM((scen_local, window, flight_local), F32),
            pltpu.VMEM((n_col, scen_local, 16, side), BF16),
            pltpu.VMEM((scenarios, col_tiles, side), BF16),
            pltpu.VMEM((scenarios, row_tiles, side), BF16),
            pltpu.VMEM((n_col, row_tiles, side), BF16),
            pltpu.VMEM((row_tiles, side), F32),
            pltpu.VMEM((row_tiles, side), F32),
            pltpu.VMEM((row_tiles, side), BF16),
            pltpu.VMEM((scenarios, row_tiles, side), BF16),
            dma((LOAD_CHUNKS,)),
            dma((1,)),
            dma((devices,)),
            dma((devices,)),
            dma((devices,)),
            dma((n_col,)),
            dma((n_col,)),
            dma((n_col,)),
        ],
        compiler_params=pltpu.CompilerParams(
            collective_id=0, has_side_effects=True, vmem_limit_bytes=48 * 1024 * 1024
        ),
    )(
        tile_values.reshape(tiles, side, side),
        row_index,
        col_place,
        row_index.reshape(1, tiles),
        col_place.reshape(1, tiles),
        increments,
        dual_vars,
        flight_cost,
        win_start.reshape(1, flight_local),
        win_len.reshape(1, flight_local),
        capacity,
    )


def solution(mesh):
    placed = (
        P("row", "col", None, None, None),
        P("row", "col", None),
        P("row", "col", None),
        P("row", None, "col"),
        P(None, "row"),
        P(None, "col"),
        P("col"),
        P("col"),
        P(None, "row"),
    )
    return jax.shard_map(
        per_device,
        mesh=mesh,
        in_specs=placed,
        out_specs=(P("row", None, "col"), P(None, "row")),
        check_vma=False,
    )
```

```python
import functools
import math
import types

import jax
import jax.numpy as jnp
from jax import lax
from jax.experimental import pallas as pl
from jax.experimental.pallas import tpu as pltpu
from jax.sharding import PartitionSpec as P

ITERS = 2
SIGMA_STEP = 0.2
PARTS = 2
GROUP = 32
MESH = pl.DeviceIdType.MESH
F32, BF16 = jnp.float32, jnp.bfloat16


def kernel(dims, names, *refs):
    n_row, n_col, scenarios, scen_local, window, tiles, row_tiles, col_tiles = dims
    ref = types.SimpleNamespace(**dict(zip(names, refs)))
    devices = n_row * n_col
    scen_part, local_part = scenarios // PARTS, scen_local // PARTS
    half_rows = row_tiles // 2
    block_rows = 16
    flights = ref.inc.shape[2]
    flight_tiles = flights * n_col // 128
    tau_step = 0.6 / math.sqrt(window)
    me_r, me_c = lax.axis_index("row"), lax.axis_index("col")
    me = me_r * n_col + me_c
    me_chip, me_core = me_c // 2, lax.rem(me_c, 2)
    parts = range(PARTS)

    def of_part(name):
        return [getattr(ref, f"{name}{part}") for part in parts]

    by_tile, slope_send, slope_recv = of_part("by_tile"), of_part("slope_send"), of_part("slope_recv")
    probe_send, probe_recv = of_part("probe_send"), of_part("probe_recv")
    image_send, image_recv = of_part("image_send"), of_part("image_recv")
    duals_recv = of_part("duals_recv")
    by_row = [b.reshape(b.shape[0] * b.shape[1], b.shape[2]) for b in by_tile]
    products = ref.products
    flat = products.reshape(products.shape[0] * products.shape[1], products.shape[2])

    def scenario_of(part, position):
        if PARTS == 1:
            return position
        return scen_local * position + part

    def load(source, target, index):
        return pltpu.make_async_copy(source, target, ref.load_sem.at[index])

    cap_lanes = pl.ds(pl.multiple_of(me_core * half_rows * 128, half_rows * 128), half_rows * 128)
    loads = [
        load(ref.dual_hbm, ref.dual_in, 0),
        load(ref.rows_hbm, ref.row_of, 1),
        load(ref.cols_hbm, ref.col_of, 2),
        load(ref.rows_hbm, ref.row_vec, 3),
        load(ref.cols_hbm, ref.col_vec, 4),
        load(ref.inc_hbm, ref.inc, 5),
        load(ref.cost_hbm, ref.cost, 6),
        load(ref.start_hbm, ref.start, 7),
        load(ref.len_hbm, ref.len, 8),
        load(ref.cap_hbm.at[:, cap_lanes], ref.cap_in, 9),
    ]

    def load_blocks(chunk):
        span = pl.ds(chunk * GROUP, GROUP)
        return pltpu.make_async_copy(
            ref.values_hbm.at[span], ref.blocks.at[span], ref.block_sem.at[chunk]
        )

    for copy in loads[:5]:
        copy.start()
    for chunk in range(tiles // GROUP):
        load_blocks(chunk).start()
    for copy in loads[5:]:
        copy.start()

    def peer_of(step):
        peer = lax.rem(me + step, devices)
        return peer // n_col, lax.rem(peer, n_col)

    barrier = pltpu.get_barrier_semaphore()

    @pl.loop(1, devices)
    def _(step):
        pl.semaphore_signal(barrier, inc=1, device_id=peer_of(step), device_id_type=MESH)

    def remote(source, target, send_sem, recv_sem, peer):
        return pltpu.make_async_remote_copy(
            src_ref=source,
            dst_ref=target,
            send_sem=send_sem,
            recv_sem=recv_sem,
            device_id=peer,
            device_id_type=MESH,
        )

    def place(buffer, r, c):
        return buffer.at[
            pl.ds(r * local_part, local_part),
            pl.ds(pl.multiple_of(c * block_rows, block_rows), block_rows),
        ]

    def slope_copy(part, peer):
        return remote(
            place(slope_send[part], *peer),
            slope_recv[part].at[me],
            ref.slope_send_sem.at[part],
            ref.slope_sem.at[part],
            peer,
        )

    def probe_copy(part, peer):
        return remote(
            probe_send[part].at[peer[1]],
            place(probe_recv[part], me_r, me_c),
            ref.probe_send_sem.at[part],
            ref.probe_sem.at[part],
            peer,
        )

    def all_blocks(part, send_sem, recv_sem):
        span = slope_recv[part].at[pl.ds(0, devices - 1)]
        return remote(span, span, send_sem.at[part], recv_sem.at[part], peer_of(1))

    def own_place(buffer, c):
        return buffer.at[
            pl.ds((c // 2) * local_part, local_part),
            pl.ds(pl.multiple_of(lax.rem(c, 2) * half_rows, half_rows), half_rows),
        ]

    def image_copy(part, step):
        peer_c = lax.rem(me_c + step, n_col)
        return remote(
            own_place(image_send[part], peer_c),
            image_recv[part].at[n_col - 1 - step],
            ref.image_send_sem.at[part],
            ref.image_sem.at[part],
            (me_r, peer_c),
        )

    def dual_copy(part, step):
        peer_c = lax.rem(me_c + step, n_col)
        return remote(
            own_place(duals_recv[part], me_c),
            own_place(duals_recv[part], me_c),
            ref.dual_send_sem.at[part],
            ref.dual_sem.at[part],
            (me_r, peer_c),
        )

    def all_rows(part, send_sem, recv_sem):
        span = image_recv[part]
        return remote(
            span, span, send_sem.at[part], recv_sem.at[part], (me_r, lax.rem(me_c + 1, n_col))
        )

    def total(triangle, values):
        return jnp.dot(
            triangle, values, precision=lax.Precision.HIGHEST, preferred_element_type=F32
        )

    def pair(part, index_of, n, transposed):
        left = jnp.concatenate(
            [by_tile[part][index_of(n)], by_tile[part][index_of(n + 1)]], axis=0
        ).astype(BF16)
        if transposed:
            right = ref.blocks[pl.ds(n, 2)].reshape(256, 128)
            contract = (((1,), (1,)), ((), ()))
        else:
            right = jnp.concatenate([ref.blocks[n], ref.blocks[n + 1]], axis=1)
            contract = (((1,), (0,)), ((), ()))
        both = lax.dot_general(left, right, contract, preferred_element_type=F32)
        products[n] = both[:scen_part, :128]
        products[n + 1] = both[scen_part:, 128:]

    def row_index(n):
        return ref.row_of[0, n]

    def col_index(n):
        tile = ref.col_of[0, n]
        return lax.rem(tile, flight_tiles) * 8 + tile // flight_tiles

    def multiply(part, index_of, transposed, loading=False):
        @pl.loop(0, tiles // GROUP)
        def _(group):
            if loading:
                load_blocks(group).wait()
            for k in range(0, GROUP, 2):
                pair(part, index_of, group * GROUP + k, transposed)

    def gathered(hot, position):
        both = jnp.concatenate(
            [flat[pl.ds(position + k, tiles, stride=scen_part), :] for k in range(2)], axis=1
        )
        high = both.astype(BF16)
        low = (both - high.astype(F32)).astype(BF16)
        return jnp.dot(
            hot[...], jnp.concatenate([high, low], axis=0), preferred_element_type=F32
        )

    def send_slope(part, sweep):
        if sweep:
            all_blocks(part, ref.slope_send_sem, ref.slope_sem).wait_send()
        for position in range(0, scen_part, 2):
            summed = gathered(ref.hot_cols, position).astype(BF16)
            slope_send[part][position] = summed[:, :128]
            slope_send[part][position + 1] = summed[:, 128:]
        if sweep == 0 and part == 0:
            pl.semaphore_wait(barrier, devices - 1)

        @pl.loop(1, devices)
        def _(step):
            slope_copy(part, peer_of(step)).start()

        slope_recv[part][me] = place(slope_send[part], me_r, me_c)[...]

    def update_primal(part, sweep, upper, running, trailing):
        all_blocks(part, ref.slope_send_sem, ref.slope_sem).wait_recv()

        @pl.loop(0, n_col)
        def _(block):
            summed = slope_recv[part][block].astype(F32)
            for group in range(1, n_row):
                summed = summed + slope_recv[part][group * n_col + block].astype(F32)
            rows = pl.ds(pl.multiple_of(block * 8, 8), 8)
            for k in range(local_part):
                for half in range(flights // 128):
                    lanes = slice(half * 128, (half + 1) * 128)
                    ref.slope[k, rows, lanes] = (
                        summed[k, half * 8 : (half + 1) * 8] + ref.cost[rows, lanes]
                    )

        if sweep:
            all_blocks(part, ref.probe_send_sem, ref.probe_sem).wait_send()
        for k in range(local_part):
            scen = part * local_part + k
            before = ref.inc if sweep == 0 else ref.primal
            gradient = total(trailing, ref.slope[k])
            fresh = jnp.clip(before[scen] - tau_step * gradient, 0.0, upper)
            ref.primal[scen] = fresh
            fresh_sum = total(running, fresh)
            probe = 2.0 * fresh_sum - ref.cumulative[scen]
            ref.cumulative[scen] = fresh_sum
            for block in range(n_col):
                probe_send[part][block, k] = jnp.concatenate(
                    [
                        probe[block * 8 : (block + 1) * 8, half * 128 : (half + 1) * 128]
                        for half in range(flights // 128)
                    ],
                    axis=0,
                ).astype(BF16)

        @pl.loop(1, devices)
        def _(step):
            probe_copy(part, peer_of(step)).start()

        place(probe_recv[part], me_r, me_c)[...] = probe_send[part][me_c]

    def send_image(part, sweep):
        all_blocks(part, ref.probe_send_sem, ref.probe_sem).wait_recv()
        for position in range(scen_part):
            by_row[part][pl.ds(position, col_tiles, stride=scen_part), :] = probe_recv[part][
                position
            ].astype(F32)
        multiply(part, col_index, True)
        if sweep:
            all_rows(part, ref.image_send_sem, ref.image_sem).wait_send()
        for position in range(0, scen_part, 2):
            summed = gathered(ref.hot_rows, position).astype(BF16)
            image_send[part][position] = summed[:, :128]
            image_send[part][position + 1] = summed[:, 128:]

        @pl.loop(1, n_col)
        def _(step):
            image_copy(part, step).start()

    def update_duals(part, sweep):
        all_rows(part, ref.image_send_sem, ref.image_sem).wait_recv()
        image = own_place(image_send[part], me_c)[...].astype(F32)
        for block in range(n_col - 1):
            image = image + image_recv[part][block].astype(F32)
        updated = jnp.maximum(
            ref.own_dual[part] + SIGMA_STEP * (image - ref.own_cap[part]), 0.0
        )
        ref.own_dual[part] = updated
        if sweep:
            all_rows(part, ref.dual_send_sem, ref.dual_sem).wait_send()
        own_place(duals_recv[part], me_c)[...] = updated.astype(BF16)

        @pl.loop(1, n_col)
        def _(step):
            dual_copy(part, step).start()

    def receive_duals(part):
        all_rows(part, ref.dual_send_sem, ref.dual_sem).wait_recv()

    loads[0].wait()

    @pl.loop(0, row_tiles // 8)
    def _(group):
        for k in range(8):
            tile = group * 8 + k
            ref.staged[pl.ds(pl.multiple_of(tile * scenarios, scenarios), scenarios), :] = (
                ref.dual_in[:, pl.ds(pl.multiple_of(tile * 128, 128), 128)]
            )

    for part in parts:
        by_row[part][0 : row_tiles * scen_part, :] = ref.staged[
            pl.ds(part, row_tiles * scen_part, stride=PARTS), :
        ]
        for k in range(local_part):
            first = me_core * half_rows * scenarios + scenario_of(part, me_chip * local_part + k)
            ref.own_dual[part, k] = ref.staged[pl.ds(first, half_rows, stride=scenarios), :]
    for copy in loads[1:5]:
        copy.wait()
    where_col = lax.rem(ref.col_vec[...], flight_tiles) * 8 + ref.col_vec[...] // flight_tiles
    hot = (where_col == lax.broadcasted_iota(jnp.int32, (col_tiles, tiles), 0)).astype(F32)
    ref.hot_cols[...] = jnp.concatenate([hot, hot], axis=1).astype(BF16)

    for part in parts:
        multiply(part, row_index, False, loading=part == 0)
        send_slope(part, 0)

    hot = (
        ref.row_vec[...] == lax.broadcasted_iota(jnp.int32, (row_tiles, tiles), 0)
    ).astype(F32)
    ref.hot_rows[...] = jnp.concatenate([hot, hot], axis=1).astype(BF16)
    for copy in loads[5:]:
        copy.wait()

    @pl.loop(0, half_rows // 8)
    def _(group):
        for k in range(8):
            tile = group * 8 + k
            ref.staged[pl.ds(pl.multiple_of(tile * scenarios, scenarios), scenarios), :] = (
                ref.cap_in[:, pl.ds(pl.multiple_of(tile * 128, 128), 128)].astype(F32)
            )

    for part in parts:
        for k in range(local_part):
            first = scenario_of(part, me_chip * local_part + k)
            ref.own_cap[part, k] = ref.staged[pl.ds(first, half_rows, stride=scenarios), :]

    row_iota = lax.broadcasted_iota(jnp.int32, (window, window), 0)
    col_iota = lax.broadcasted_iota(jnp.int32, (window, window), 1)
    running = (row_iota >= col_iota).astype(F32)
    trailing = (row_iota <= col_iota).astype(F32)
    for scen in range(scen_local):
        ref.cumulative[scen] = total(running, ref.inc[scen])
    minutes = lax.broadcasted_iota(jnp.int32, (window, flights), 0)
    upper = (
        (minutes >= ref.start[...]) & (minutes < ref.start[...] + ref.len[...])
    ).astype(F32)

    for sweep in range(ITERS):
        for part in parts:
            update_primal(part, sweep, upper, running, trailing)
        for part in parts:
            send_image(part, sweep)
        for part in parts:
            update_duals(part, sweep)
        for part in parts:
            receive_duals(part)
            for position in range(scen_part):
                if sweep < ITERS - 1:
                    target, rows = by_row[part], pl.ds(position, row_tiles, stride=scen_part)
                else:
                    target = ref.staged
                    rows = pl.ds(scenario_of(part, position), row_tiles, stride=scenarios)
                target[rows, :] = duals_recv[part][position].astype(F32)
            if sweep < ITERS - 1:
                multiply(part, row_index, False)
                send_slope(part, sweep + 1)

    @pl.loop(0, row_tiles // 8)
    def _(group):
        for k in range(8):
            tile = group * 8 + k
            ref.duals[:, pl.ds(pl.multiple_of(tile * 128, 128), 128)] = ref.staged[
                pl.ds(pl.multiple_of(tile * scenarios, scenarios), scenarios), :
            ]

    for part in parts:
        all_blocks(part, ref.slope_send_sem, ref.slope_sem).wait_send()
        all_blocks(part, ref.probe_send_sem, ref.probe_sem).wait_send()
        all_rows(part, ref.image_send_sem, ref.image_sem).wait_send()
        all_rows(part, ref.dual_send_sem, ref.dual_sem).wait_send()


def per_device(
    tile_values,
    tile_rows,
    tile_cols,
    increments,
    dual_vars,
    flight_cost,
    win_start,
    win_len,
    capacity,
):
    n_row, n_col = lax.axis_size("row"), lax.axis_size("col")
    tiles, side = tile_values.shape[2], tile_values.shape[3]
    scen_local, window, flight_local = increments.shape
    scenarios, row_length = dual_vars.shape
    row_tiles = row_length // side
    time_block = window // n_col
    col_tiles = time_block * flight_local * n_col // side
    devices = n_row * n_col
    scen_part, local_part = scenarios // PARTS, scen_local // PARTS
    assert side == 128 and time_block == 8 and flight_local == 256
    assert scenarios == n_col and scen_local == 2
    dims = (n_row, n_col, scenarios, scen_local, window, tiles, row_tiles, col_tiles)
    vmem = pl.BlockSpec(memory_space=pltpu.VMEM)
    inputs = dict(
        values_hbm=tile_values.reshape(tiles, side, side),
        rows_hbm=tile_rows.reshape(1, tiles),
        cols_hbm=tile_cols.reshape(1, tiles),
        inc_hbm=increments,
        dual_hbm=dual_vars,
        cost_hbm=flight_cost,
        start_hbm=win_start.reshape(1, flight_local),
        len_hbm=win_len.reshape(1, flight_local),
        cap_hbm=capacity,
    )
    dma = pltpu.SemaphoreType.DMA
    scratch = dict(
        row_of=pltpu.SMEM((1, tiles), jnp.int32),
        col_of=pltpu.SMEM((1, tiles), jnp.int32),
        row_vec=pltpu.VMEM((1, tiles), jnp.int32),
        col_vec=pltpu.VMEM((1, tiles), jnp.int32),
        inc=pltpu.VMEM(increments.shape, F32),
        dual_in=pltpu.VMEM(dual_vars.shape, F32),
        cost=pltpu.VMEM(flight_cost.shape, F32),
        start=pltpu.VMEM((1, flight_local), jnp.int32),
        len=pltpu.VMEM((1, flight_local), jnp.int32),
        cap_in=pltpu.VMEM((scenarios, row_length // 2), jnp.int32),
        blocks=pltpu.VMEM((tiles, side, side), BF16),
        hot_cols=pltpu.VMEM((col_tiles, 2 * tiles), BF16),
        hot_rows=pltpu.VMEM((row_tiles, 2 * tiles), BF16),
        products=pltpu.VMEM((tiles, scen_part, side), F32),
        staged=pltpu.VMEM((row_tiles * scenarios, side), F32),
        slope=pltpu.VMEM((local_part, window, flight_local), F32),
        cumulative=pltpu.VMEM(increments.shape, F32),
        own_dual=pltpu.VMEM((PARTS, local_part, row_tiles // 2, side), F32),
        own_cap=pltpu.VMEM((PARTS, local_part, row_tiles // 2, side), F32),
        load_sem=dma((10,)),
        block_sem=dma((tiles // GROUP,)),
        slope_send_sem=dma((PARTS,)),
        slope_sem=dma((PARTS,)),
        probe_send_sem=dma((PARTS,)),
        probe_sem=dma((PARTS,)),
        image_send_sem=dma((PARTS,)),
        image_sem=dma((PARTS,)),
        dual_send_sem=dma((PARTS,)),
        dual_sem=dma((PARTS,)),
    )
    for part in range(PARTS):
        scratch.update(
            {
                f"by_tile{part}": pltpu.VMEM((max(col_tiles, row_tiles), scen_part, side), F32),
                f"slope_send{part}": pltpu.VMEM((scen_part, col_tiles, side), BF16),
                f"slope_recv{part}": pltpu.VMEM((devices, local_part, 16, side), BF16),
                f"probe_send{part}": pltpu.VMEM((n_col, local_part, 16, side), BF16),
                f"probe_recv{part}": pltpu.VMEM((scen_part, col_tiles, side), BF16),
                f"image_send{part}": pltpu.VMEM((scen_part, row_tiles, side), BF16),
                f"image_recv{part}": pltpu.VMEM((n_col - 1, local_part, row_tiles // 2, side), BF16),
                f"duals_recv{part}": pltpu.VMEM((scen_part, row_tiles, side), BF16),
            }
        )
    names = tuple(inputs) + ("primal", "duals") + tuple(scratch)
    return pl.pallas_call(
        functools.partial(kernel, dims, names),
        out_shape=(
            jax.ShapeDtypeStruct(increments.shape, F32),
            jax.ShapeDtypeStruct(dual_vars.shape, F32),
        ),
        in_specs=[pl.BlockSpec(memory_space=pl.ANY)] * len(inputs),
        out_specs=(vmem, vmem),
        scratch_shapes=list(scratch.values()),
        compiler_params=pltpu.CompilerParams(
            collective_id=0, has_side_effects=True, vmem_limit_bytes=56 * 1024 * 1024
        ),
    )(*inputs.values())


def solution(mesh):
    placed = (
        P("row", "col", None, None, None),
        P("row", "col", None),
        P("row", "col", None),
        P("row", None, "col"),
        P(None, "row"),
        P(None, "col"),
        P("col"),
        P("col"),
        P(None, "row"),
    )
    return jax.shard_map(
        per_device,
        mesh=mesh,
        in_specs=placed,
        out_specs=(P("row", None, "col"), P(None, "row")),
        check_vma=False,
    )
```

```python
import functools
import itertools
import math
import types

import jax
import jax.numpy as jnp
from jax import lax
from jax.experimental import pallas as pl
from jax.experimental.pallas import tpu as pltpu
from jax.sharding import PartitionSpec as P

ITERS = 2
SIGMA_STEP = 0.2
PARTS = 2
GROUP = 64
MESH = pl.DeviceIdType.MESH
F32, BF16 = jnp.float32, jnp.bfloat16


def kernel(dims, names, *refs):
    n_row, n_col, scenarios, scen_local, window, tiles, row_tiles, col_tiles = dims
    ref = types.SimpleNamespace(**dict(zip(names, refs)))
    devices = n_row * n_col
    scen_part, local_part = scenarios // PARTS, scen_local // PARTS
    half_rows = row_tiles // 2
    block_rows = 16
    flights = ref.inc.shape[2]
    flight_tiles = flights * n_col // 128
    tau_step = 0.6 / math.sqrt(window)
    me_r, me_c = lax.axis_index("row"), lax.axis_index("col")
    me = me_r * n_col + me_c
    me_chip, me_core = me_c // 2, lax.rem(me_c, 2)
    assert (n_row, n_col) == (8, 16)
    parts = range(PARTS)

    def of_part(name):
        return [getattr(ref, f"{name}{part}") for part in parts]

    by_tile, slope_send, slope_recv = of_part("by_tile"), of_part("slope_send"), of_part("slope_recv")
    probe_send, probe_recv = of_part("probe_send"), of_part("probe_recv")
    image_send, image_recv = of_part("image_send"), of_part("image_recv")
    duals_recv = of_part("duals_recv")
    by_row = [b.reshape(b.shape[0] * b.shape[1], b.shape[2]) for b in by_tile]
    products = ref.products
    flat = products.reshape(products.shape[0] * products.shape[1], products.shape[2])

    def scenario_of(part, position):
        if PARTS == 1:
            return position
        return scen_local * position + part

    def load(source, target, index):
        return pltpu.make_async_copy(source, target, ref.load_sem.at[index])

    cap_lanes = pl.ds(pl.multiple_of(me_core * half_rows * 128, half_rows * 128), half_rows * 128)
    loads = [
        load(ref.dual_hbm, ref.dual_in, 0),
        load(ref.rows_hbm, ref.row_of, 1),
        load(ref.cols_hbm, ref.col_of, 2),
        load(ref.rows_hbm, ref.row_vec, 3),
        load(ref.cols_hbm, ref.col_vec, 4),
        load(ref.inc_hbm, ref.inc, 5),
        load(ref.cost_hbm, ref.cost, 6),
        load(ref.start_hbm, ref.start, 7),
        load(ref.len_hbm, ref.len, 8),
        load(ref.cap_hbm.at[:, cap_lanes], ref.cap_in, 9),
    ]

    def load_blocks(chunk):
        span = pl.ds(chunk * GROUP, GROUP)
        return pltpu.make_async_copy(
            ref.values_hbm.at[span], ref.blocks.at[span], ref.block_sem.at[chunk]
        )

    for copy in loads[:5]:
        copy.start()
    for chunk in range(tiles // GROUP):
        load_blocks(chunk).start()
    for copy in loads[5:]:
        copy.start()

    me_z, me_y = me_r // 2, lax.rem(me_chip, 4)
    me_x = (me_chip // 4) * 2 + lax.rem(me_r, 2)
    along_x = [lax.rem(me_x + d, 4) for d in range(4)]
    row_z = [lax.rem(me_z + d, 4) * 2 for d in range(4)]
    row_x = [lax.rem(x, 2) for x in along_x]
    col_x = [(x // 2) * 8 for x in along_x]
    col_y = [lax.rem(me_y + d, 4) * 2 for d in range(4)]
    col_core = [me_core, 1 - me_core]

    def hops(offset):
        return sum(min(d, 4 - d) for d in offset[:-1]) + offset[-1] / 8

    def farthest_first(*sizes):
        return sorted(itertools.product(*map(range, sizes)), key=hops, reverse=True)[:-1]

    every_peer = [
        (row_z[dz] + row_x[dx], col_x[dx] + col_y[dy] + col_core[dc])
        for dz, dx, dy, dc in farthest_first(4, 4, 4, 2)
    ]
    row_peers = [
        (me_r, col_x[dx] + col_y[dy] + col_core[dc])
        for dx, dy, dc in sorted(
            ((2 * far, dy, dc) for far in range(2) for dy in range(4) for dc in range(2)),
            key=hops,
            reverse=True,
        )[:-1]
    ]

    barrier = pltpu.get_barrier_semaphore()

    for peer in every_peer:
        pl.semaphore_signal(barrier, inc=1, device_id=peer, device_id_type=MESH)

    def remote(source, target, send_sem, recv_sem, peer):
        return pltpu.make_async_remote_copy(
            src_ref=source,
            dst_ref=target,
            send_sem=send_sem,
            recv_sem=recv_sem,
            device_id=peer,
            device_id_type=MESH,
        )

    def place(buffer, r, c):
        return buffer.at[
            pl.ds(r * local_part, local_part),
            pl.ds(pl.multiple_of(c * block_rows, block_rows), block_rows),
        ]

    def slope_copy(part, peer):
        return remote(
            place(slope_send[part], *peer),
            slope_recv[part].at[me],
            ref.slope_send_sem.at[part],
            ref.slope_sem.at[part],
            peer,
        )

    def probe_copy(part, peer):
        return remote(
            probe_send[part].at[peer[1]],
            place(probe_recv[part], me_r, me_c),
            ref.probe_send_sem.at[part],
            ref.probe_sem.at[part],
            peer,
        )

    def all_blocks(part, send_sem, recv_sem):
        span = slope_recv[part].at[pl.ds(0, devices - 1)]
        return remote(span, span, send_sem.at[part], recv_sem.at[part], every_peer[0])

    def own_place(buffer, c):
        return buffer.at[
            pl.ds((c // 2) * local_part, local_part),
            pl.ds(pl.multiple_of(lax.rem(c, 2) * half_rows, half_rows), half_rows),
        ]

    def image_copy(part, index):
        return remote(
            own_place(image_send[part], row_peers[index][1]),
            image_recv[part].at[index],
            ref.image_send_sem.at[part],
            ref.image_sem.at[part],
            row_peers[index],
        )

    def dual_copy(part, index):
        return remote(
            own_place(duals_recv[part], me_c),
            own_place(duals_recv[part], me_c),
            ref.dual_send_sem.at[part],
            ref.dual_sem.at[part],
            row_peers[index],
        )

    def all_rows(part, send_sem, recv_sem):
        span = image_recv[part]
        return remote(span, span, send_sem.at[part], recv_sem.at[part], row_peers[0])

    def total(triangle, values):
        return jnp.dot(
            triangle, values, precision=lax.Precision.HIGHEST, preferred_element_type=F32
        )

    def pair(part, index_of, n, transposed):
        left = jnp.concatenate(
            [by_tile[part][index_of(n)], by_tile[part][index_of(n + 1)]], axis=0
        ).astype(BF16)
        if transposed:
            right = ref.blocks[pl.ds(n, 2)].reshape(256, 128)
            contract = (((1,), (1,)), ((), ()))
        else:
            right = jnp.concatenate([ref.blocks[n], ref.blocks[n + 1]], axis=1)
            contract = (((1,), (0,)), ((), ()))
        both = lax.dot_general(left, right, contract, preferred_element_type=F32)
        products[n] = both[:scen_part, :128]
        products[n + 1] = both[scen_part:, 128:]

    def row_index(n):
        return ref.row_of[0, n]

    def col_index(n):
        tile = ref.col_of[0, n]
        return lax.rem(tile, flight_tiles) * 8 + tile // flight_tiles

    def multiply(part, index_of, transposed, loading=False):
        @pl.loop(0, tiles // GROUP)
        def _(group):
            if loading:
                load_blocks(group).wait()
            for k in range(0, GROUP, 2):
                pair(part, index_of, group * GROUP + k, transposed)

    def gathered(hot, position):
        both = jnp.concatenate(
            [flat[pl.ds(position + k, tiles, stride=scen_part), :] for k in range(2)], axis=1
        )
        high = both.astype(BF16)
        low = (both - high.astype(F32)).astype(BF16)
        return jnp.dot(
            hot[...], jnp.concatenate([high, low], axis=0), preferred_element_type=F32
        )

    def fold_slope(part, sweep):
        if sweep:
            all_blocks(part, ref.slope_send_sem, ref.slope_sem).wait_send()
        for position in range(0, scen_part, 2):
            summed = gathered(ref.hot_cols, position).astype(BF16)
            slope_send[part][position] = summed[:, :128]
            slope_send[part][position + 1] = summed[:, 128:]

    def send_slope(part):
        for peer in every_peer:
            slope_copy(part, peer).start()
        slope_recv[part][me] = place(slope_send[part], me_r, me_c)[...]

    def update_primal(part, sweep, upper, running, trailing):
        all_blocks(part, ref.slope_send_sem, ref.slope_sem).wait_recv()

        @pl.loop(0, n_col)
        def _(block):
            summed = slope_recv[part][block].astype(F32)
            for group in range(1, n_row):
                summed = summed + slope_recv[part][group * n_col + block].astype(F32)
            rows = pl.ds(pl.multiple_of(block * 8, 8), 8)
            for k in range(local_part):
                for half in range(flights // 128):
                    lanes = slice(half * 128, (half + 1) * 128)
                    ref.slope[k, rows, lanes] = (
                        summed[k, half * 8 : (half + 1) * 8] + ref.cost[rows, lanes]
                    )

        if sweep:
            all_blocks(part, ref.probe_send_sem, ref.probe_sem).wait_send()
        for k in range(local_part):
            scen = part * local_part + k
            before = ref.inc if sweep == 0 else ref.primal
            gradient = total(trailing, ref.slope[k])
            fresh = jnp.clip(before[scen] - tau_step * gradient, 0.0, upper)
            ref.primal[scen] = fresh
            fresh_sum = total(running, fresh)
            probe = 2.0 * fresh_sum - ref.cumulative[scen]
            ref.cumulative[scen] = fresh_sum
            for block in range(n_col):
                probe_send[part][block, k] = jnp.concatenate(
                    [
                        probe[block * 8 : (block + 1) * 8, half * 128 : (half + 1) * 128]
                        for half in range(flights // 128)
                    ],
                    axis=0,
                ).astype(BF16)

        for peer in every_peer:
            probe_copy(part, peer).start()

        place(probe_recv[part], me_r, me_c)[...] = probe_send[part][me_c]

    def send_image(part, sweep):
        all_blocks(part, ref.probe_send_sem, ref.probe_sem).wait_recv()
        for position in range(scen_part):
            by_row[part][pl.ds(position, col_tiles, stride=scen_part), :] = probe_recv[part][
                position
            ].astype(F32)
        multiply(part, col_index, True)
        if sweep:
            all_rows(part, ref.image_send_sem, ref.image_sem).wait_send()
        for position in range(0, scen_part, 2):
            summed = gathered(ref.hot_rows, position).astype(BF16)
            image_send[part][position] = summed[:, :128]
            image_send[part][position + 1] = summed[:, 128:]

        for index in range(n_col - 1):
            image_copy(part, index).start()

    def update_duals(part, sweep):
        all_rows(part, ref.image_send_sem, ref.image_sem).wait_recv()
        image = own_place(image_send[part], me_c)[...].astype(F32)
        for block in range(n_col - 1):
            image = image + image_recv[part][block].astype(F32)
        updated = jnp.maximum(
            ref.own_dual[part] + SIGMA_STEP * (image - ref.own_cap[part]), 0.0
        )
        ref.own_dual[part] = updated
        if sweep:
            all_rows(part, ref.dual_send_sem, ref.dual_sem).wait_send()
        own_place(duals_recv[part], me_c)[...] = updated.astype(BF16)

        for index in range(n_col - 1):
            dual_copy(part, index).start()

    def receive_duals(part):
        all_rows(part, ref.dual_send_sem, ref.dual_sem).wait_recv()

    loads[0].wait()

    @pl.loop(0, row_tiles // 8)
    def _(group):
        for k in range(8):
            tile = group * 8 + k
            ref.staged[pl.ds(pl.multiple_of(tile * scenarios, scenarios), scenarios), :] = (
                ref.dual_in[:, pl.ds(pl.multiple_of(tile * 128, 128), 128)]
            )

    for part in parts:
        by_row[part][0 : row_tiles * scen_part, :] = ref.staged[
            pl.ds(part, row_tiles * scen_part, stride=PARTS), :
        ]
        for k in range(local_part):
            first = me_core * half_rows * scenarios + scenario_of(part, me_chip * local_part + k)
            ref.own_dual[part, k] = ref.staged[pl.ds(first, half_rows, stride=scenarios), :]
    for copy in loads[1:5]:
        copy.wait()
    where_col = lax.rem(ref.col_vec[...], flight_tiles) * 8 + ref.col_vec[...] // flight_tiles
    hot = (where_col == lax.broadcasted_iota(jnp.int32, (col_tiles, tiles), 0)).astype(F32)
    ref.hot_cols[...] = jnp.concatenate([hot, hot], axis=1).astype(BF16)

    for part in parts:
        multiply(part, row_index, False, loading=part == 0)
        fold_slope(part, 0)
        if part == 0:
            pl.semaphore_wait(barrier, devices - 1)
        send_slope(part)

    hot = (
        ref.row_vec[...] == lax.broadcasted_iota(jnp.int32, (row_tiles, tiles), 0)
    ).astype(F32)
    ref.hot_rows[...] = jnp.concatenate([hot, hot], axis=1).astype(BF16)
    for copy in loads[5:]:
        copy.wait()

    @pl.loop(0, half_rows // 8)
    def _(group):
        for k in range(8):
            tile = group * 8 + k
            ref.staged[pl.ds(pl.multiple_of(tile * scenarios, scenarios), scenarios), :] = (
                ref.cap_in[:, pl.ds(pl.multiple_of(tile * 128, 128), 128)].astype(F32)
            )

    for part in parts:
        for k in range(local_part):
            first = scenario_of(part, me_chip * local_part + k)
            ref.own_cap[part, k] = ref.staged[pl.ds(first, half_rows, stride=scenarios), :]

    row_iota = lax.broadcasted_iota(jnp.int32, (window, window), 0)
    col_iota = lax.broadcasted_iota(jnp.int32, (window, window), 1)
    running = (row_iota >= col_iota).astype(F32)
    trailing = (row_iota <= col_iota).astype(F32)
    for scen in range(scen_local):
        ref.cumulative[scen] = total(running, ref.inc[scen])
    minutes = lax.broadcasted_iota(jnp.int32, (window, flights), 0)
    upper = (
        (minutes >= ref.start[...]) & (minutes < ref.start[...] + ref.len[...])
    ).astype(F32)

    for sweep in range(ITERS):
        for part in parts:
            update_primal(part, sweep, upper, running, trailing)
        for part in parts:
            send_image(part, sweep)
        for part in parts:
            update_duals(part, sweep)
        for part in parts:
            receive_duals(part)
            for position in range(scen_part):
                if sweep < ITERS - 1:
                    target, rows = by_row[part], pl.ds(position, row_tiles, stride=scen_part)
                else:
                    target = ref.staged
                    rows = pl.ds(scenario_of(part, position), row_tiles, stride=scenarios)
                target[rows, :] = duals_recv[part][position].astype(F32)
            if sweep < ITERS - 1:
                multiply(part, row_index, False)
                fold_slope(part, sweep + 1)
                send_slope(part)

    @pl.loop(0, row_tiles // 8)
    def _(group):
        for k in range(8):
            tile = group * 8 + k
            ref.duals[:, pl.ds(pl.multiple_of(tile * 128, 128), 128)] = ref.staged[
                pl.ds(pl.multiple_of(tile * scenarios, scenarios), scenarios), :
            ]

    for part in parts:
        all_blocks(part, ref.slope_send_sem, ref.slope_sem).wait_send()
        all_blocks(part, ref.probe_send_sem, ref.probe_sem).wait_send()
        all_rows(part, ref.image_send_sem, ref.image_sem).wait_send()
        all_rows(part, ref.dual_send_sem, ref.dual_sem).wait_send()


def per_device(
    tile_values,
    tile_rows,
    tile_cols,
    increments,
    dual_vars,
    flight_cost,
    win_start,
    win_len,
    capacity,
):
    n_row, n_col = lax.axis_size("row"), lax.axis_size("col")
    tiles, side = tile_values.shape[2], tile_values.shape[3]
    scen_local, window, flight_local = increments.shape
    scenarios, row_length = dual_vars.shape
    row_tiles = row_length // side
    time_block = window // n_col
    col_tiles = time_block * flight_local * n_col // side
    devices = n_row * n_col
    scen_part, local_part = scenarios // PARTS, scen_local // PARTS
    assert side == 128 and time_block == 8 and flight_local == 256
    assert scenarios == n_col and scen_local == 2
    dims = (n_row, n_col, scenarios, scen_local, window, tiles, row_tiles, col_tiles)
    vmem = pl.BlockSpec(memory_space=pltpu.VMEM)
    inputs = dict(
        values_hbm=tile_values.reshape(tiles, side, side),
        rows_hbm=tile_rows.reshape(1, tiles),
        cols_hbm=tile_cols.reshape(1, tiles),
        inc_hbm=increments,
        dual_hbm=dual_vars,
        cost_hbm=flight_cost,
        start_hbm=win_start.reshape(1, flight_local),
        len_hbm=win_len.reshape(1, flight_local),
        cap_hbm=capacity,
    )
    dma = pltpu.SemaphoreType.DMA
    scratch = dict(
        row_of=pltpu.SMEM((1, tiles), jnp.int32),
        col_of=pltpu.SMEM((1, tiles), jnp.int32),
        row_vec=pltpu.VMEM((1, tiles), jnp.int32),
        col_vec=pltpu.VMEM((1, tiles), jnp.int32),
        inc=pltpu.VMEM(increments.shape, F32),
        dual_in=pltpu.VMEM(dual_vars.shape, F32),
        cost=pltpu.VMEM(flight_cost.shape, F32),
        start=pltpu.VMEM((1, flight_local), jnp.int32),
        len=pltpu.VMEM((1, flight_local), jnp.int32),
        cap_in=pltpu.VMEM((scenarios, row_length // 2), jnp.int32),
        blocks=pltpu.VMEM((tiles, side, side), BF16),
        hot_cols=pltpu.VMEM((col_tiles, 2 * tiles), BF16),
        hot_rows=pltpu.VMEM((row_tiles, 2 * tiles), BF16),
        products=pltpu.VMEM((tiles, scen_part, side), F32),
        staged=pltpu.VMEM((row_tiles * scenarios, side), F32),
        slope=pltpu.VMEM((local_part, window, flight_local), F32),
        cumulative=pltpu.VMEM(increments.shape, F32),
        own_dual=pltpu.VMEM((PARTS, local_part, row_tiles // 2, side), F32),
        own_cap=pltpu.VMEM((PARTS, local_part, row_tiles // 2, side), F32),
        load_sem=dma((10,)),
        block_sem=dma((tiles // GROUP,)),
        slope_send_sem=dma((PARTS,)),
        slope_sem=dma((PARTS,)),
        probe_send_sem=dma((PARTS,)),
        probe_sem=dma((PARTS,)),
        image_send_sem=dma((PARTS,)),
        image_sem=dma((PARTS,)),
        dual_send_sem=dma((PARTS,)),
        dual_sem=dma((PARTS,)),
    )
    for part in range(PARTS):
        scratch.update(
            {
                f"by_tile{part}": pltpu.VMEM((max(col_tiles, row_tiles), scen_part, side), F32),
                f"slope_send{part}": pltpu.VMEM((scen_part, col_tiles, side), BF16),
                f"slope_recv{part}": pltpu.VMEM((devices, local_part, 16, side), BF16),
                f"probe_send{part}": pltpu.VMEM((n_col, local_part, 16, side), BF16),
                f"probe_recv{part}": pltpu.VMEM((scen_part, col_tiles, side), BF16),
                f"image_send{part}": pltpu.VMEM((scen_part, row_tiles, side), BF16),
                f"image_recv{part}": pltpu.VMEM((n_col - 1, local_part, row_tiles // 2, side), BF16),
                f"duals_recv{part}": pltpu.VMEM((scen_part, row_tiles, side), BF16),
            }
        )
    names = tuple(inputs) + ("primal", "duals") + tuple(scratch)
    return pl.pallas_call(
        functools.partial(kernel, dims, names),
        out_shape=(
            jax.ShapeDtypeStruct(increments.shape, F32),
            jax.ShapeDtypeStruct(dual_vars.shape, F32),
        ),
        in_specs=[pl.BlockSpec(memory_space=pl.ANY)] * len(inputs),
        out_specs=(vmem, vmem),
        scratch_shapes=list(scratch.values()),
        compiler_params=pltpu.CompilerParams(
            collective_id=0, has_side_effects=True, vmem_limit_bytes=56 * 1024 * 1024
        ),
    )(*inputs.values())


def solution(mesh):
    placed = (
        P("row", "col", None, None, None),
        P("row", "col", None),
        P("row", "col", None),
        P("row", None, "col"),
        P(None, "row"),
        P(None, "col"),
        P("col"),
        P("col"),
        P(None, "row"),
    )
    return jax.shard_map(
        per_device,
        mesh=mesh,
        in_specs=placed,
        out_specs=(P("row", None, "col"), P(None, "row")),
        check_vma=False,
    )
```

```python
import functools
import itertools
import math
import types

import jax
import jax.numpy as jnp
from jax import lax
from jax.experimental import pallas as pl
from jax.experimental.pallas import tpu as pltpu
from jax.sharding import PartitionSpec as P

ITERS = 2
SIGMA_STEP = 0.2
PARTS = 2
GROUP = 64
MESH = pl.DeviceIdType.MESH
F32, BF16 = jnp.float32, jnp.bfloat16


def kernel(dims, names, *refs):
    n_row, n_col, scenarios, scen_local, window, tiles, row_tiles, col_tiles = dims
    ref = types.SimpleNamespace(**dict(zip(names, refs)))
    devices = n_row * n_col
    scen_part, local_part = scenarios // PARTS, scen_local // PARTS
    half_rows = row_tiles // 2
    block_rows = 16
    flights = ref.inc.shape[2]
    flight_tiles = flights * n_col // 128
    tau_step = 0.6 / math.sqrt(window)
    me_r, me_c = lax.axis_index("row"), lax.axis_index("col")
    me = me_r * n_col + me_c
    me_chip, me_core = me_c // 2, lax.rem(me_c, 2)
    assert (n_row, n_col) == (8, 16)
    parts = range(PARTS)

    def of_part(name):
        return [getattr(ref, f"{name}{part}") for part in parts]

    by_tile, slope_send, slope_recv = of_part("by_tile"), of_part("slope_send"), of_part("slope_recv")
    probe_send, probe_recv = of_part("probe_send"), of_part("probe_recv")
    image_send, image_recv = of_part("image_send"), of_part("image_recv")
    duals_recv = of_part("duals_recv")
    by_row = [b.reshape(b.shape[0] * b.shape[1], b.shape[2]) for b in by_tile]
    products = of_part("products")
    flat = [p.reshape(p.shape[0] * p.shape[1], p.shape[2]) for p in products]

    def scenario_of(part, position):
        if PARTS == 1:
            return position
        return scen_local * position + part

    def load(source, target, index):
        return pltpu.make_async_copy(source, target, ref.load_sem.at[index])

    cap_lanes = pl.ds(pl.multiple_of(me_core * half_rows * 128, half_rows * 128), half_rows * 128)
    loads = [
        load(ref.dual_hbm, ref.dual_in, 0),
        load(ref.rows_hbm, ref.row_of, 1),
        load(ref.cols_hbm, ref.col_of, 2),
        load(ref.rows_hbm, ref.row_vec, 3),
        load(ref.cols_hbm, ref.col_vec, 4),
        load(ref.inc_hbm, ref.inc, 5),
        load(ref.cost_hbm, ref.cost, 6),
        load(ref.start_hbm, ref.start, 7),
        load(ref.len_hbm, ref.len, 8),
        load(ref.cap_hbm.at[:, cap_lanes], ref.cap_in, 9),
    ]

    def load_blocks(chunk):
        span = pl.ds(chunk * GROUP, GROUP)
        return pltpu.make_async_copy(
            ref.values_hbm.at[span], ref.blocks.at[span], ref.block_sem.at[chunk]
        )

    for copy in loads[:5]:
        copy.start()
    for chunk in range(tiles // GROUP):
        load_blocks(chunk).start()
    for copy in loads[5:]:
        copy.start()

    me_z, me_y = me_r // 2, lax.rem(me_chip, 4)
    me_x = (me_chip // 4) * 2 + lax.rem(me_r, 2)
    along_x = [lax.rem(me_x + d, 4) for d in range(4)]
    row_z = [lax.rem(me_z + d, 4) * 2 for d in range(4)]
    row_x = [lax.rem(x, 2) for x in along_x]
    col_x = [(x // 2) * 8 for x in along_x]
    col_y = [lax.rem(me_y + d, 4) * 2 for d in range(4)]
    col_core = [me_core, 1 - me_core]

    def hops(offset):
        return sum(min(d, 4 - d) for d in offset[:-1]) + offset[-1] / 8

    def farthest_first(*sizes):
        return sorted(itertools.product(*map(range, sizes)), key=hops, reverse=True)[:-1]

    every_peer = [
        (row_z[dz] + row_x[dx], col_x[dx] + col_y[dy] + col_core[dc])
        for dz, dx, dy, dc in farthest_first(4, 4, 4, 2)
    ]
    row_peers = [
        (me_r, col_x[dx] + col_y[dy] + col_core[dc])
        for dx, dy, dc in sorted(
            ((2 * far, dy, dc) for far in range(2) for dy in range(4) for dc in range(2)),
            key=hops,
            reverse=True,
        )[:-1]
    ]

    barrier = pltpu.get_barrier_semaphore()

    for peer in every_peer:
        pl.semaphore_signal(barrier, inc=1, device_id=peer, device_id_type=MESH)

    def remote(source, target, send_sem, recv_sem, peer):
        return pltpu.make_async_remote_copy(
            src_ref=source,
            dst_ref=target,
            send_sem=send_sem,
            recv_sem=recv_sem,
            device_id=peer,
            device_id_type=MESH,
        )

    def place(buffer, r, c):
        return buffer.at[
            pl.ds(r * local_part, local_part),
            pl.ds(pl.multiple_of(c * block_rows, block_rows), block_rows),
        ]

    def slope_copy(part, peer):
        return remote(
            place(slope_send[part], *peer),
            slope_recv[part].at[me],
            ref.slope_send_sem.at[part],
            ref.slope_sem.at[part],
            peer,
        )

    def probe_copy(part, peer):
        return remote(
            probe_send[part].at[peer[1]],
            place(probe_recv[part], me_r, me_c),
            ref.probe_send_sem.at[part],
            ref.probe_sem.at[part],
            peer,
        )

    def all_blocks(part, send_sem, recv_sem):
        span = slope_recv[part].at[pl.ds(0, devices - 1)]
        return remote(span, span, send_sem.at[part], recv_sem.at[part], every_peer[0])

    def own_place(buffer, c):
        return buffer.at[
            pl.ds((c // 2) * local_part, local_part),
            pl.ds(pl.multiple_of(lax.rem(c, 2) * half_rows, half_rows), half_rows),
        ]

    def image_copy(part, index):
        return remote(
            own_place(image_send[part], row_peers[index][1]),
            image_recv[part].at[index],
            ref.image_send_sem.at[part],
            ref.image_sem.at[part],
            row_peers[index],
        )

    def dual_copy(part, index):
        return remote(
            own_place(duals_recv[part], me_c),
            own_place(duals_recv[part], me_c),
            ref.dual_send_sem.at[part],
            ref.dual_sem.at[part],
            row_peers[index],
        )

    def all_rows(part, send_sem, recv_sem):
        span = image_recv[part]
        return remote(span, span, send_sem.at[part], recv_sem.at[part], row_peers[0])

    def total(triangle, values):
        return jnp.dot(
            triangle, values, precision=lax.Precision.HIGHEST, preferred_element_type=F32
        )

    def pair(part, index_of, n, transposed):
        left = jnp.concatenate(
            [by_tile[part][index_of(n)], by_tile[part][index_of(n + 1)]], axis=0
        ).astype(BF16)
        if transposed:
            right = ref.blocks[pl.ds(n, 2)].reshape(256, 128)
            contract = (((1,), (1,)), ((), ()))
        else:
            right = jnp.concatenate([ref.blocks[n], ref.blocks[n + 1]], axis=1)
            contract = (((1,), (0,)), ((), ()))
        both = lax.dot_general(left, right, contract, preferred_element_type=F32)
        products[part][n] = both[:scen_part, :128]
        products[part][n + 1] = both[scen_part:, 128:]

    def row_index(n):
        return ref.row_of[0, n]

    def col_index(n):
        tile = ref.col_of[0, n]
        return lax.rem(tile, flight_tiles) * 8 + tile // flight_tiles

    def multiply(part, index_of, transposed):
        @pl.loop(0, tiles // GROUP)
        def _(group):
            for k in range(0, GROUP, 2):
                pair(part, index_of, group * GROUP + k, transposed)

    def multiply_arriving():
        @pl.loop(0, tiles // GROUP)
        def _(group):
            load_blocks(group).wait()
            for k in range(0, GROUP, 2):
                n = group * GROUP + k
                left = jnp.concatenate(
                    [by_tile[part][row_index(n + i)] for i in range(2) for part in parts], axis=0
                ).astype(BF16)
                right = jnp.concatenate([ref.blocks[n], ref.blocks[n + 1]], axis=1)
                both = jnp.dot(left, right, preferred_element_type=F32)
                for i in range(2):
                    for part in parts:
                        first = i * scenarios + part * scen_part
                        products[part][n + i] = both[
                            first : first + scen_part, i * 128 : (i + 1) * 128
                        ]

    def gathered(part, hot, position):
        both = jnp.concatenate(
            [flat[part][pl.ds(position + k, tiles, stride=scen_part), :] for k in range(2)], axis=1
        )
        high = both.astype(BF16)
        low = (both - high.astype(F32)).astype(BF16)
        return jnp.dot(
            hot[...], jnp.concatenate([high, low], axis=0), preferred_element_type=F32
        )

    def fold_slope(part, sweep):
        if sweep:
            all_blocks(part, ref.slope_send_sem, ref.slope_sem).wait_send()
        for position in range(0, scen_part, 2):
            summed = gathered(part, ref.hot_cols, position).astype(BF16)
            slope_send[part][position] = summed[:, :128]
            slope_send[part][position + 1] = summed[:, 128:]

    def send_slope(part):
        for peer in every_peer:
            slope_copy(part, peer).start()
        slope_recv[part][me] = place(slope_send[part], me_r, me_c)[...]

    def update_primal(part, sweep, upper, running, trailing):
        all_blocks(part, ref.slope_send_sem, ref.slope_sem).wait_recv()

        @pl.loop(0, n_col, unroll=4)
        def _(block):
            summed = slope_recv[part][block].astype(F32)
            for group in range(1, n_row):
                summed = summed + slope_recv[part][group * n_col + block].astype(F32)
            rows = pl.ds(pl.multiple_of(block * 8, 8), 8)
            for k in range(local_part):
                for half in range(flights // 128):
                    lanes = slice(half * 128, (half + 1) * 128)
                    ref.slope[k, rows, lanes] = (
                        summed[k, half * 8 : (half + 1) * 8] + ref.cost[rows, lanes]
                    )

        if sweep:
            all_blocks(part, ref.probe_send_sem, ref.probe_sem).wait_send()
        for k in range(local_part):
            scen = part * local_part + k
            before = ref.inc if sweep == 0 else ref.primal
            gradient = total(trailing, ref.slope[k])
            fresh = jnp.clip(before[scen] - tau_step * gradient, 0.0, upper)
            ref.primal[scen] = fresh
            fresh_sum = total(running, fresh)
            probe = 2.0 * fresh_sum - ref.cumulative[scen]
            ref.cumulative[scen] = fresh_sum
            for block in range(n_col):
                probe_send[part][block, k] = jnp.concatenate(
                    [
                        probe[block * 8 : (block + 1) * 8, half * 128 : (half + 1) * 128]
                        for half in range(flights // 128)
                    ],
                    axis=0,
                ).astype(BF16)

        for peer in every_peer:
            probe_copy(part, peer).start()

        place(probe_recv[part], me_r, me_c)[...] = probe_send[part][me_c]

    def send_image(part, sweep):
        all_blocks(part, ref.probe_send_sem, ref.probe_sem).wait_recv()
        for position in range(scen_part):
            by_row[part][pl.ds(position, col_tiles, stride=scen_part), :] = probe_recv[part][
                position
            ].astype(F32)
        multiply(part, col_index, True)
        if sweep:
            all_rows(part, ref.image_send_sem, ref.image_sem).wait_send()
        for position in range(0, scen_part, 2):
            summed = gathered(part, ref.hot_rows, position).astype(BF16)
            image_send[part][position] = summed[:, :128]
            image_send[part][position + 1] = summed[:, 128:]

        for index in range(n_col - 1):
            image_copy(part, index).start()

    def update_duals(part, sweep):
        all_rows(part, ref.image_send_sem, ref.image_sem).wait_recv()
        image = own_place(image_send[part], me_c)[...].astype(F32)
        for block in range(n_col - 1):
            image = image + image_recv[part][block].astype(F32)
        updated = jnp.maximum(
            ref.own_dual[part] + SIGMA_STEP * (image - ref.own_cap[part]), 0.0
        )
        ref.own_dual[part] = updated
        if sweep:
            all_rows(part, ref.dual_send_sem, ref.dual_sem).wait_send()
        own_place(duals_recv[part], me_c)[...] = updated.astype(BF16)

        for index in range(n_col - 1):
            dual_copy(part, index).start()

    def receive_duals(part):
        all_rows(part, ref.dual_send_sem, ref.dual_sem).wait_recv()

    loads[0].wait()

    @pl.loop(0, row_tiles // 8)
    def _(group):
        for k in range(8):
            tile = group * 8 + k
            ref.staged[pl.ds(pl.multiple_of(tile * scenarios, scenarios), scenarios), :] = (
                ref.dual_in[:, pl.ds(pl.multiple_of(tile * 128, 128), 128)]
            )

    for part in parts:
        by_row[part][0 : row_tiles * scen_part, :] = ref.staged[
            pl.ds(part, row_tiles * scen_part, stride=PARTS), :
        ]
        for k in range(local_part):
            first = me_core * half_rows * scenarios + scenario_of(part, me_chip * local_part + k)
            ref.own_dual[part, k] = ref.staged[pl.ds(first, half_rows, stride=scenarios), :]
    for copy in loads[1:5]:
        copy.wait()
    where_col = lax.rem(ref.col_vec[...], flight_tiles) * 8 + ref.col_vec[...] // flight_tiles
    hot = (where_col == lax.broadcasted_iota(jnp.int32, (col_tiles, tiles), 0)).astype(F32)
    ref.hot_cols[...] = jnp.concatenate([hot, hot], axis=1).astype(BF16)

    multiply_arriving()
    for part in parts:
        fold_slope(part, 0)
        if part == 0:
            pl.semaphore_wait(barrier, devices - 1)
        send_slope(part)

    hot = (
        ref.row_vec[...] == lax.broadcasted_iota(jnp.int32, (row_tiles, tiles), 0)
    ).astype(F32)
    ref.hot_rows[...] = jnp.concatenate([hot, hot], axis=1).astype(BF16)
    for copy in loads[5:]:
        copy.wait()

    @pl.loop(0, half_rows // 8)
    def _(group):
        for k in range(8):
            tile = group * 8 + k
            ref.staged[pl.ds(pl.multiple_of(tile * scenarios, scenarios), scenarios), :] = (
                ref.cap_in[:, pl.ds(pl.multiple_of(tile * 128, 128), 128)].astype(F32)
            )

    for part in parts:
        for k in range(local_part):
            first = scenario_of(part, me_chip * local_part + k)
            ref.own_cap[part, k] = ref.staged[pl.ds(first, half_rows, stride=scenarios), :]

    row_iota = lax.broadcasted_iota(jnp.int32, (window, window), 0)
    col_iota = lax.broadcasted_iota(jnp.int32, (window, window), 1)
    running = (row_iota >= col_iota).astype(F32)
    trailing = (row_iota <= col_iota).astype(F32)
    for scen in range(scen_local):
        ref.cumulative[scen] = total(running, ref.inc[scen])
    minutes = lax.broadcasted_iota(jnp.int32, (window, flights), 0)
    upper = (
        (minutes >= ref.start[...]) & (minutes < ref.start[...] + ref.len[...])
    ).astype(F32)

    for sweep in range(ITERS):
        for part in parts:
            update_primal(part, sweep, upper, running, trailing)
        for part in parts:
            send_image(part, sweep)
        for part in parts:
            update_duals(part, sweep)
        for part in parts:
            receive_duals(part)
            for position in range(scen_part):
                if sweep < ITERS - 1:
                    target, rows = by_row[part], pl.ds(position, row_tiles, stride=scen_part)
                else:
                    target = ref.staged
                    rows = pl.ds(scenario_of(part, position), row_tiles, stride=scenarios)
                target[rows, :] = duals_recv[part][position].astype(F32)
            if sweep < ITERS - 1:
                multiply(part, row_index, False)
                fold_slope(part, sweep + 1)
                send_slope(part)

    @pl.loop(0, row_tiles // 8)
    def _(group):
        for k in range(8):
            tile = group * 8 + k
            ref.duals[:, pl.ds(pl.multiple_of(tile * 128, 128), 128)] = ref.staged[
                pl.ds(pl.multiple_of(tile * scenarios, scenarios), scenarios), :
            ]

    for part in parts:
        all_blocks(part, ref.slope_send_sem, ref.slope_sem).wait_send()
        all_blocks(part, ref.probe_send_sem, ref.probe_sem).wait_send()
        all_rows(part, ref.image_send_sem, ref.image_sem).wait_send()
        all_rows(part, ref.dual_send_sem, ref.dual_sem).wait_send()


def per_device(
    tile_values,
    tile_rows,
    tile_cols,
    increments,
    dual_vars,
    flight_cost,
    win_start,
    win_len,
    capacity,
):
    n_row, n_col = lax.axis_size("row"), lax.axis_size("col")
    tiles, side = tile_values.shape[2], tile_values.shape[3]
    scen_local, window, flight_local = increments.shape
    scenarios, row_length = dual_vars.shape
    row_tiles = row_length // side
    time_block = window // n_col
    col_tiles = time_block * flight_local * n_col // side
    devices = n_row * n_col
    scen_part, local_part = scenarios // PARTS, scen_local // PARTS
    assert side == 128 and time_block == 8 and flight_local == 256
    assert scenarios == n_col and scen_local == 2
    dims = (n_row, n_col, scenarios, scen_local, window, tiles, row_tiles, col_tiles)
    vmem = pl.BlockSpec(memory_space=pltpu.VMEM)
    inputs = dict(
        values_hbm=tile_values.reshape(tiles, side, side),
        rows_hbm=tile_rows.reshape(1, tiles),
        cols_hbm=tile_cols.reshape(1, tiles),
        inc_hbm=increments,
        dual_hbm=dual_vars,
        cost_hbm=flight_cost,
        start_hbm=win_start.reshape(1, flight_local),
        len_hbm=win_len.reshape(1, flight_local),
        cap_hbm=capacity,
    )
    dma = pltpu.SemaphoreType.DMA
    scratch = dict(
        row_of=pltpu.SMEM((1, tiles), jnp.int32),
        col_of=pltpu.SMEM((1, tiles), jnp.int32),
        row_vec=pltpu.VMEM((1, tiles), jnp.int32),
        col_vec=pltpu.VMEM((1, tiles), jnp.int32),
        inc=pltpu.VMEM(increments.shape, F32),
        dual_in=pltpu.VMEM(dual_vars.shape, F32),
        cost=pltpu.VMEM(flight_cost.shape, F32),
        start=pltpu.VMEM((1, flight_local), jnp.int32),
        len=pltpu.VMEM((1, flight_local), jnp.int32),
        cap_in=pltpu.VMEM((scenarios, row_length // 2), jnp.int32),
        blocks=pltpu.VMEM((tiles, side, side), BF16),
        hot_cols=pltpu.VMEM((col_tiles, 2 * tiles), BF16),
        hot_rows=pltpu.VMEM((row_tiles, 2 * tiles), BF16),
        staged=pltpu.VMEM((row_tiles * scenarios, side), F32),
        slope=pltpu.VMEM((local_part, window, flight_local), F32),
        cumulative=pltpu.VMEM(increments.shape, F32),
        own_dual=pltpu.VMEM((PARTS, local_part, row_tiles // 2, side), F32),
        own_cap=pltpu.VMEM((PARTS, local_part, row_tiles // 2, side), F32),
        load_sem=dma((10,)),
        block_sem=dma((tiles // GROUP,)),
        slope_send_sem=dma((PARTS,)),
        slope_sem=dma((PARTS,)),
        probe_send_sem=dma((PARTS,)),
        probe_sem=dma((PARTS,)),
        image_send_sem=dma((PARTS,)),
        image_sem=dma((PARTS,)),
        dual_send_sem=dma((PARTS,)),
        dual_sem=dma((PARTS,)),
    )
    for part in range(PARTS):
        scratch.update(
            {
                f"by_tile{part}": pltpu.VMEM((max(col_tiles, row_tiles), scen_part, side), F32),
                f"products{part}": pltpu.VMEM((tiles, scen_part, side), F32),
                f"slope_send{part}": pltpu.VMEM((scen_part, col_tiles, side), BF16),
                f"slope_recv{part}": pltpu.VMEM((devices, local_part, 16, side), BF16),
                f"probe_send{part}": pltpu.VMEM((n_col, local_part, 16, side), BF16),
                f"probe_recv{part}": pltpu.VMEM((scen_part, col_tiles, side), BF16),
                f"image_send{part}": pltpu.VMEM((scen_part, row_tiles, side), BF16),
                f"image_recv{part}": pltpu.VMEM((n_col - 1, local_part, row_tiles // 2, side), BF16),
                f"duals_recv{part}": pltpu.VMEM((scen_part, row_tiles, side), BF16),
            }
        )
    names = tuple(inputs) + ("primal", "duals") + tuple(scratch)
    return pl.pallas_call(
        functools.partial(kernel, dims, names),
        out_shape=(
            jax.ShapeDtypeStruct(increments.shape, F32),
            jax.ShapeDtypeStruct(dual_vars.shape, F32),
        ),
        in_specs=[pl.BlockSpec(memory_space=pl.ANY)] * len(inputs),
        out_specs=(vmem, vmem),
        scratch_shapes=list(scratch.values()),
        compiler_params=pltpu.CompilerParams(
            collective_id=0, has_side_effects=True, vmem_limit_bytes=56 * 1024 * 1024
        ),
    )(*inputs.values())


def solution(mesh):
    placed = (
        P("row", "col", None, None, None),
        P("row", "col", None),
        P("row", "col", None),
        P("row", None, "col"),
        P(None, "row"),
        P(None, "col"),
        P("col"),
        P("col"),
        P(None, "row"),
    )
    return jax.shard_map(
        per_device,
        mesh=mesh,
        in_specs=placed,
        out_specs=(P("row", None, "col"), P(None, "row")),
        check_vma=False,
    )
```

```python
import functools
import itertools
import math
import types

import jax
import jax.numpy as jnp
from jax import lax
from jax.experimental import pallas as pl
from jax.experimental.pallas import tpu as pltpu
from jax.sharding import PartitionSpec as P

ITERS = 2
SIGMA_STEP = 0.2
PARTS = 2
GROUP = 64
MESH = pl.DeviceIdType.MESH
F32, BF16 = jnp.float32, jnp.bfloat16


def kernel(dims, names, *refs):
    n_row, n_col, scenarios, scen_local, window, tiles, row_tiles, col_tiles = dims
    ref = types.SimpleNamespace(**dict(zip(names, refs)))
    devices = n_row * n_col
    scen_part, local_part = scenarios // PARTS, scen_local // PARTS
    half_rows = row_tiles // 2
    block_rows = 16
    flights = ref.inc.shape[2]
    flight_tiles = flights * n_col // 128
    tau_step = 0.6 / math.sqrt(window)
    me_r, me_c = lax.axis_index("row"), lax.axis_index("col")
    me = me_r * n_col + me_c
    me_chip, me_core = me_c // 2, lax.rem(me_c, 2)
    assert (n_row, n_col) == (8, 16)
    parts = range(PARTS)

    def of_part(name):
        return [getattr(ref, f"{name}{part}") for part in parts]

    by_tile, slope_send, slope_recv = of_part("by_tile"), of_part("slope_send"), of_part("slope_recv")
    probe_send, probe_recv = of_part("probe_send"), of_part("probe_recv")
    image_send, image_recv = of_part("image_send"), of_part("image_recv")
    duals_recv = of_part("duals_recv")
    by_row = [b.reshape(b.shape[0] * b.shape[1], b.shape[2]) for b in by_tile]
    products = of_part("products")
    flat = [p.reshape(p.shape[0] * p.shape[1], p.shape[2]) for p in products]

    def scenario_of(part, position):
        if PARTS == 1:
            return position
        return scen_local * position + part

    def load(source, target, index):
        return pltpu.make_async_copy(source, target, ref.load_sem.at[index])

    cap_lanes = pl.ds(pl.multiple_of(me_core * half_rows * 128, half_rows * 128), half_rows * 128)
    loads = [
        load(ref.dual_hbm, ref.dual_in, 0),
        load(ref.rows_hbm, ref.row_of, 1),
        load(ref.cols_hbm, ref.col_of, 2),
        load(ref.rows_hbm, ref.row_vec, 3),
        load(ref.cols_hbm, ref.col_vec, 4),
        load(ref.inc_hbm, ref.inc, 5),
        load(ref.cost_hbm, ref.cost, 6),
        load(ref.start_hbm, ref.start, 7),
        load(ref.len_hbm, ref.len, 8),
        load(ref.cap_hbm.at[:, cap_lanes], ref.cap_in, 9),
    ]

    def load_blocks(chunk):
        span = pl.ds(chunk * GROUP, GROUP)
        return pltpu.make_async_copy(
            ref.values_hbm.at[span], ref.blocks.at[span], ref.block_sem.at[chunk]
        )

    for copy in loads[:5]:
        copy.start()
    for chunk in range(tiles // GROUP):
        load_blocks(chunk).start()
    for copy in loads[5:]:
        copy.start()

    me_z, me_y = me_r // 2, lax.rem(me_chip, 4)
    me_x = (me_chip // 4) * 2 + lax.rem(me_r, 2)
    along_x = [lax.rem(me_x + d, 4) for d in range(4)]
    row_z = [lax.rem(me_z + d, 4) * 2 for d in range(4)]
    row_x = [lax.rem(x, 2) for x in along_x]
    col_x = [(x // 2) * 8 for x in along_x]
    col_y = [lax.rem(me_y + d, 4) * 2 for d in range(4)]
    col_core = [me_core, 1 - me_core]

    def hops(offset):
        return sum(min(d, 4 - d) for d in offset[:-1]) + offset[-1] / 8

    def farthest_first(*sizes):
        return sorted(itertools.product(*map(range, sizes)), key=hops, reverse=True)[:-1]

    every_peer = [
        (row_z[dz] + row_x[dx], col_x[dx] + col_y[dy] + col_core[dc])
        for dz, dx, dy, dc in farthest_first(4, 4, 4, 2)
    ]
    row_peers = [
        (me_r, col_x[dx] + col_y[dy] + col_core[dc])
        for dx, dy, dc in sorted(
            ((2 * far, dy, dc) for far in range(2) for dy in range(4) for dc in range(2)),
            key=hops,
            reverse=True,
        )[:-1]
    ]

    barrier = pltpu.get_barrier_semaphore()

    for peer in every_peer:
        pl.semaphore_signal(barrier, inc=1, device_id=peer, device_id_type=MESH)

    def remote(source, target, send_sem, recv_sem, peer):
        return pltpu.make_async_remote_copy(
            src_ref=source,
            dst_ref=target,
            send_sem=send_sem,
            recv_sem=recv_sem,
            device_id=peer,
            device_id_type=MESH,
        )

    def place(buffer, r, c):
        return buffer.at[
            pl.ds(r * local_part, local_part),
            pl.ds(pl.multiple_of(c * block_rows, block_rows), block_rows),
        ]

    def slope_copy(part, peer):
        return remote(
            place(slope_send[part], *peer),
            slope_recv[part].at[me],
            ref.slope_send_sem.at[part],
            ref.slope_sem.at[part],
            peer,
        )

    def probe_copy(part, peer):
        return remote(
            probe_send[part].at[peer[1]],
            place(probe_recv[part], me_r, me_c),
            ref.probe_send_sem.at[part],
            ref.probe_sem.at[part],
            peer,
        )

    def all_blocks(part, send_sem, recv_sem):
        span = slope_recv[part].at[pl.ds(0, devices - 1)]
        return remote(span, span, send_sem.at[part], recv_sem.at[part], every_peer[0])

    def own_place(buffer, c):
        return buffer.at[
            pl.ds((c // 2) * local_part, local_part),
            pl.ds(pl.multiple_of(lax.rem(c, 2) * half_rows, half_rows), half_rows),
        ]

    def image_copy(part, index):
        return remote(
            own_place(image_send[part], row_peers[index][1]),
            image_recv[part].at[index],
            ref.image_send_sem.at[part],
            ref.image_sem.at[part],
            row_peers[index],
        )

    def dual_copy(part, index):
        return remote(
            own_place(duals_recv[part], me_c),
            own_place(duals_recv[part], me_c),
            ref.dual_send_sem.at[part],
            ref.dual_sem.at[part],
            row_peers[index],
        )

    def all_rows(part, send_sem, recv_sem):
        span = image_recv[part]
        return remote(span, span, send_sem.at[part], recv_sem.at[part], row_peers[0])

    def total(triangle, values):
        return jnp.dot(
            triangle, values, precision=lax.Precision.HIGHEST, preferred_element_type=F32
        )

    def pair(part, index_of, n, transposed):
        left = jnp.concatenate(
            [by_tile[part][index_of(n)], by_tile[part][index_of(n + 1)]], axis=0
        ).astype(BF16)
        if transposed:
            right = ref.blocks[pl.ds(n, 2)].reshape(256, 128)
            contract = (((1,), (1,)), ((), ()))
        else:
            right = jnp.concatenate([ref.blocks[n], ref.blocks[n + 1]], axis=1)
            contract = (((1,), (0,)), ((), ()))
        both = lax.dot_general(left, right, contract, preferred_element_type=F32)
        products[part][n] = both[:scen_part, :128]
        products[part][n + 1] = both[scen_part:, 128:]

    def row_index(n):
        return ref.row_of[0, n]

    def col_index(n):
        tile = ref.col_of[0, n]
        return lax.rem(tile, flight_tiles) * 8 + tile // flight_tiles

    def multiply(part, index_of, transposed):
        @pl.loop(0, tiles // GROUP)
        def _(group):
            for k in range(0, GROUP, 2):
                pair(part, index_of, group * GROUP + k, transposed)

    def multiply_arriving():
        @pl.loop(0, tiles // GROUP)
        def _(group):
            load_blocks(group).wait()
            for k in range(0, GROUP, 2):
                n = group * GROUP + k
                left = jnp.concatenate(
                    [by_tile[part][row_index(n + i)] for i in range(2) for part in parts], axis=0
                ).astype(BF16)
                right = jnp.concatenate([ref.blocks[n], ref.blocks[n + 1]], axis=1)
                both = jnp.dot(left, right, preferred_element_type=F32)
                for i in range(2):
                    for part in parts:
                        first = i * scenarios + part * scen_part
                        products[part][n + i] = both[
                            first : first + scen_part, i * 128 : (i + 1) * 128
                        ]

    def gathered(part, hot, position):
        both = jnp.concatenate(
            [flat[part][pl.ds(position + k, tiles, stride=scen_part), :] for k in range(2)], axis=1
        )
        high = both.astype(BF16)
        low = (both - high.astype(F32)).astype(BF16)
        return jnp.dot(
            hot[...], jnp.concatenate([high, low], axis=0), preferred_element_type=F32
        )

    def fold_slope(part, sweep):
        if sweep:
            all_blocks(part, ref.slope_send_sem, ref.slope_sem).wait_send()
        for position in range(0, scen_part, 2):
            summed = gathered(part, ref.hot_cols, position)
            ref.shaped[:col_tiles] = summed[:, :128]
            ref.shaped[col_tiles:] = summed[:, 128:]
            carried = jnp.zeros((2 * col_tiles // 8, 128), F32)
            for minute in reversed(range(8)):
                rows = pl.ds(minute, 2 * col_tiles // 8, stride=8)
                exact = ref.shaped[rows, :] + carried
                rounded = exact.astype(BF16).astype(F32)
                ref.shaped[rows, :] = rounded
                carried = exact - rounded
            slope_send[part][position] = ref.shaped[:col_tiles].astype(BF16)
            slope_send[part][position + 1] = ref.shaped[col_tiles:].astype(BF16)

    def send_slope(part):
        for peer in every_peer:
            slope_copy(part, peer).start()
        slope_recv[part][me] = place(slope_send[part], me_r, me_c)[...]

    def update_primal(part, sweep, upper, running, trailing):
        all_blocks(part, ref.slope_send_sem, ref.slope_sem).wait_recv()

        @pl.loop(0, n_col, unroll=4)
        def _(block):
            summed = slope_recv[part][block].astype(F32)
            for group in range(1, n_row):
                summed = summed + slope_recv[part][group * n_col + block].astype(F32)
            rows = pl.ds(pl.multiple_of(block * 8, 8), 8)
            for k in range(local_part):
                for half in range(flights // 128):
                    lanes = slice(half * 128, (half + 1) * 128)
                    ref.slope[k, rows, lanes] = (
                        summed[k, half * 8 : (half + 1) * 8] + ref.cost[rows, lanes]
                    )

        if sweep:
            all_blocks(part, ref.probe_send_sem, ref.probe_sem).wait_send()
        for k in range(local_part):
            scen = part * local_part + k
            before = ref.inc if sweep == 0 else ref.primal
            gradient = total(trailing, ref.slope[k])
            fresh = jnp.clip(before[scen] - tau_step * gradient, 0.0, upper)
            ref.primal[scen] = fresh
            fresh_sum = total(running, fresh)
            probe = 2.0 * fresh_sum - ref.cumulative[scen]
            ref.cumulative[scen] = fresh_sum
            for block in range(n_col):
                probe_send[part][block, k] = jnp.concatenate(
                    [
                        probe[block * 8 : (block + 1) * 8, half * 128 : (half + 1) * 128]
                        for half in range(flights // 128)
                    ],
                    axis=0,
                ).astype(BF16)

        for peer in every_peer:
            probe_copy(part, peer).start()

        place(probe_recv[part], me_r, me_c)[...] = probe_send[part][me_c]

    def send_image(part, sweep):
        all_blocks(part, ref.probe_send_sem, ref.probe_sem).wait_recv()
        for position in range(scen_part):
            by_row[part][pl.ds(position, col_tiles, stride=scen_part), :] = probe_recv[part][
                position
            ].astype(F32)
        multiply(part, col_index, True)
        if sweep:
            all_rows(part, ref.image_send_sem, ref.image_sem).wait_send()
        for position in range(0, scen_part, 2):
            summed = gathered(part, ref.hot_rows, position).astype(BF16)
            image_send[part][position] = summed[:, :128]
            image_send[part][position + 1] = summed[:, 128:]

        for index in range(n_col - 1):
            image_copy(part, index).start()

    def update_duals(part, sweep):
        all_rows(part, ref.image_send_sem, ref.image_sem).wait_recv()
        image = own_place(image_send[part], me_c)[...].astype(F32)
        for block in range(n_col - 1):
            image = image + image_recv[part][block].astype(F32)
        updated = jnp.maximum(
            ref.own_dual[part] + SIGMA_STEP * (image - ref.own_cap[part]), 0.0
        )
        ref.own_dual[part] = updated
        if sweep:
            all_rows(part, ref.dual_send_sem, ref.dual_sem).wait_send()
        own_place(duals_recv[part], me_c)[...] = updated.astype(BF16)

        for index in range(n_col - 1):
            dual_copy(part, index).start()

    def receive_duals(part):
        all_rows(part, ref.dual_send_sem, ref.dual_sem).wait_recv()

    loads[0].wait()

    @pl.loop(0, row_tiles // 8)
    def _(group):
        for k in range(8):
            tile = group * 8 + k
            ref.staged[pl.ds(pl.multiple_of(tile * scenarios, scenarios), scenarios), :] = (
                ref.dual_in[:, pl.ds(pl.multiple_of(tile * 128, 128), 128)]
            )

    for part in parts:
        by_row[part][0 : row_tiles * scen_part, :] = ref.staged[
            pl.ds(part, row_tiles * scen_part, stride=PARTS), :
        ]
        for k in range(local_part):
            first = me_core * half_rows * scenarios + scenario_of(part, me_chip * local_part + k)
            ref.own_dual[part, k] = ref.staged[pl.ds(first, half_rows, stride=scenarios), :]
    for copy in loads[1:5]:
        copy.wait()
    where_col = lax.rem(ref.col_vec[...], flight_tiles) * 8 + ref.col_vec[...] // flight_tiles
    hot = (where_col == lax.broadcasted_iota(jnp.int32, (col_tiles, tiles), 0)).astype(F32)
    ref.hot_cols[...] = jnp.concatenate([hot, hot], axis=1).astype(BF16)

    multiply_arriving()
    for part in parts:
        fold_slope(part, 0)
        if part == 0:
            pl.semaphore_wait(barrier, devices - 1)
        send_slope(part)

    hot = (
        ref.row_vec[...] == lax.broadcasted_iota(jnp.int32, (row_tiles, tiles), 0)
    ).astype(F32)
    ref.hot_rows[...] = jnp.concatenate([hot, hot], axis=1).astype(BF16)
    for copy in loads[5:]:
        copy.wait()

    @pl.loop(0, half_rows // 8)
    def _(group):
        for k in range(8):
            tile = group * 8 + k
            ref.staged[pl.ds(pl.multiple_of(tile * scenarios, scenarios), scenarios), :] = (
                ref.cap_in[:, pl.ds(pl.multiple_of(tile * 128, 128), 128)].astype(F32)
            )

    for part in parts:
        for k in range(local_part):
            first = scenario_of(part, me_chip * local_part + k)
            ref.own_cap[part, k] = ref.staged[pl.ds(first, half_rows, stride=scenarios), :]

    row_iota = lax.broadcasted_iota(jnp.int32, (window, window), 0)
    col_iota = lax.broadcasted_iota(jnp.int32, (window, window), 1)
    running = (row_iota >= col_iota).astype(F32)
    trailing = (row_iota <= col_iota).astype(F32)
    for scen in range(scen_local):
        ref.cumulative[scen] = total(running, ref.inc[scen])
    minutes = lax.broadcasted_iota(jnp.int32, (window, flights), 0)
    upper = (
        (minutes >= ref.start[...]) & (minutes < ref.start[...] + ref.len[...])
    ).astype(F32)

    for sweep in range(ITERS):
        for part in parts:
            update_primal(part, sweep, upper, running, trailing)
        for part in parts:
            send_image(part, sweep)
        for part in parts:
            update_duals(part, sweep)
        for part in parts:
            receive_duals(part)
            for position in range(scen_part):
                if sweep < ITERS - 1:
                    target, rows = by_row[part], pl.ds(position, row_tiles, stride=scen_part)
                else:
                    target = ref.staged
                    rows = pl.ds(scenario_of(part, position), row_tiles, stride=scenarios)
                target[rows, :] = duals_recv[part][position].astype(F32)
            if sweep < ITERS - 1:
                multiply(part, row_index, False)
                fold_slope(part, sweep + 1)
                send_slope(part)

    @pl.loop(0, row_tiles // 8)
    def _(group):
        for k in range(8):
            tile = group * 8 + k
            ref.duals[:, pl.ds(pl.multiple_of(tile * 128, 128), 128)] = ref.staged[
                pl.ds(pl.multiple_of(tile * scenarios, scenarios), scenarios), :
            ]

    for part in parts:
        all_blocks(part, ref.slope_send_sem, ref.slope_sem).wait_send()
        all_blocks(part, ref.probe_send_sem, ref.probe_sem).wait_send()
        all_rows(part, ref.image_send_sem, ref.image_sem).wait_send()
        all_rows(part, ref.dual_send_sem, ref.dual_sem).wait_send()


def per_device(
    tile_values,
    tile_rows,
    tile_cols,
    increments,
    dual_vars,
    flight_cost,
    win_start,
    win_len,
    capacity,
):
    n_row, n_col = lax.axis_size("row"), lax.axis_size("col")
    tiles, side = tile_values.shape[2], tile_values.shape[3]
    scen_local, window, flight_local = increments.shape
    scenarios, row_length = dual_vars.shape
    row_tiles = row_length // side
    time_block = window // n_col
    col_tiles = time_block * flight_local * n_col // side
    devices = n_row * n_col
    scen_part, local_part = scenarios // PARTS, scen_local // PARTS
    assert side == 128 and time_block == 8 and flight_local == 256
    assert scenarios == n_col and scen_local == 2
    dims = (n_row, n_col, scenarios, scen_local, window, tiles, row_tiles, col_tiles)
    vmem = pl.BlockSpec(memory_space=pltpu.VMEM)
    inputs = dict(
        values_hbm=tile_values.reshape(tiles, side, side),
        rows_hbm=tile_rows.reshape(1, tiles),
        cols_hbm=tile_cols.reshape(1, tiles),
        inc_hbm=increments,
        dual_hbm=dual_vars,
        cost_hbm=flight_cost,
        start_hbm=win_start.reshape(1, flight_local),
        len_hbm=win_len.reshape(1, flight_local),
        cap_hbm=capacity,
    )
    dma = pltpu.SemaphoreType.DMA
    scratch = dict(
        row_of=pltpu.SMEM((1, tiles), jnp.int32),
        col_of=pltpu.SMEM((1, tiles), jnp.int32),
        row_vec=pltpu.VMEM((1, tiles), jnp.int32),
        col_vec=pltpu.VMEM((1, tiles), jnp.int32),
        inc=pltpu.VMEM(increments.shape, F32),
        dual_in=pltpu.VMEM(dual_vars.shape, F32),
        cost=pltpu.VMEM(flight_cost.shape, F32),
        start=pltpu.VMEM((1, flight_local), jnp.int32),
        len=pltpu.VMEM((1, flight_local), jnp.int32),
        cap_in=pltpu.VMEM((scenarios, row_length // 2), jnp.int32),
        blocks=pltpu.VMEM((tiles, side, side), BF16),
        hot_cols=pltpu.VMEM((col_tiles, 2 * tiles), BF16),
        hot_rows=pltpu.VMEM((row_tiles, 2 * tiles), BF16),
        shaped=pltpu.VMEM((2 * col_tiles, side), F32),
        staged=pltpu.VMEM((row_tiles * scenarios, side), F32),
        slope=pltpu.VMEM((local_part, window, flight_local), F32),
        cumulative=pltpu.VMEM(increments.shape, F32),
        own_dual=pltpu.VMEM((PARTS, local_part, row_tiles // 2, side), F32),
        own_cap=pltpu.VMEM((PARTS, local_part, row_tiles // 2, side), F32),
        load_sem=dma((10,)),
        block_sem=dma((tiles // GROUP,)),
        slope_send_sem=dma((PARTS,)),
        slope_sem=dma((PARTS,)),
        probe_send_sem=dma((PARTS,)),
        probe_sem=dma((PARTS,)),
        image_send_sem=dma((PARTS,)),
        image_sem=dma((PARTS,)),
        dual_send_sem=dma((PARTS,)),
        dual_sem=dma((PARTS,)),
    )
    for part in range(PARTS):
        scratch.update(
            {
                f"by_tile{part}": pltpu.VMEM((max(col_tiles, row_tiles), scen_part, side), F32),
                f"products{part}": pltpu.VMEM((tiles, scen_part, side), F32),
                f"slope_send{part}": pltpu.VMEM((scen_part, col_tiles, side), BF16),
                f"slope_recv{part}": pltpu.VMEM((devices, local_part, 16, side), BF16),
                f"probe_send{part}": pltpu.VMEM((n_col, local_part, 16, side), BF16),
                f"probe_recv{part}": pltpu.VMEM((scen_part, col_tiles, side), BF16),
                f"image_send{part}": pltpu.VMEM((scen_part, row_tiles, side), BF16),
                f"image_recv{part}": pltpu.VMEM((n_col - 1, local_part, row_tiles // 2, side), BF16),
                f"duals_recv{part}": pltpu.VMEM((scen_part, row_tiles, side), BF16),
            }
        )
    names = tuple(inputs) + ("primal", "duals") + tuple(scratch)
    return pl.pallas_call(
        functools.partial(kernel, dims, names),
        out_shape=(
            jax.ShapeDtypeStruct(increments.shape, F32),
            jax.ShapeDtypeStruct(dual_vars.shape, F32),
        ),
        in_specs=[pl.BlockSpec(memory_space=pl.ANY)] * len(inputs),
        out_specs=(vmem, vmem),
        scratch_shapes=list(scratch.values()),
        compiler_params=pltpu.CompilerParams(
            collective_id=0, has_side_effects=True, vmem_limit_bytes=56 * 1024 * 1024
        ),
    )(*inputs.values())


def solution(mesh):
    placed = (
        P("row", "col", None, None, None),
        P("row", "col", None),
        P("row", "col", None),
        P("row", None, "col"),
        P(None, "row"),
        P(None, "col"),
        P("col"),
        P("col"),
        P(None, "row"),
    )
    return jax.shard_map(
        per_device,
        mesh=mesh,
        in_specs=placed,
        out_specs=(P("row", None, "col"), P(None, "row")),
        check_vma=False,
    )
```

```python
import functools
import itertools
import math
import types

import jax
import jax.numpy as jnp
from jax import lax
from jax.experimental import pallas as pl
from jax.experimental.pallas import tpu as pltpu
from jax.sharding import PartitionSpec as P

ITERS = 2
SIGMA_STEP = 0.2
PARTS = 2
GROUP = 64
UNROLLED = 128
MESH = pl.DeviceIdType.MESH
F32, BF16 = jnp.float32, jnp.bfloat16


def kernel(dims, names, *refs):
    n_row, n_col, scenarios, scen_local, window, tiles, row_tiles, col_tiles = dims
    ref = types.SimpleNamespace(**dict(zip(names, refs)))
    devices = n_row * n_col
    scen_part, local_part = scenarios // PARTS, scen_local // PARTS
    half_rows = row_tiles // 2
    block_rows = 16
    flights = ref.inc.shape[2]
    flight_tiles = flights * n_col // 128
    tau_step = 0.6 / math.sqrt(window)
    me_r, me_c = lax.axis_index("row"), lax.axis_index("col")
    me = me_r * n_col + me_c
    me_chip, me_core = me_c // 2, lax.rem(me_c, 2)
    assert (n_row, n_col) == (8, 16)
    parts = range(PARTS)

    def of_part(name):
        return [getattr(ref, f"{name}{part}") for part in parts]

    by_tile, slope_send, slope_recv = of_part("by_tile"), of_part("slope_send"), of_part("slope_recv")
    probe_send, probe_recv = of_part("probe_send"), of_part("probe_recv")
    image_send, image_recv = of_part("image_send"), of_part("image_recv")
    duals_recv = of_part("duals_recv")
    by_row = [b.reshape(b.shape[0] * b.shape[1], b.shape[2]) for b in by_tile]
    products = of_part("products")
    flat = [p.reshape(p.shape[0] * p.shape[1], p.shape[2]) for p in products]

    def scenario_of(part, position):
        if PARTS == 1:
            return position
        return scen_local * position + part

    def load(source, target, index):
        return pltpu.make_async_copy(source, target, ref.load_sem.at[index])

    cap_lanes = pl.ds(pl.multiple_of(me_core * half_rows * 128, half_rows * 128), half_rows * 128)
    loads = [
        load(ref.dual_hbm, ref.dual_in, 0),
        load(ref.rows_hbm, ref.row_of, 1),
        load(ref.cols_hbm, ref.col_of, 2),
        load(ref.rows_hbm, ref.row_vec, 3),
        load(ref.cols_hbm, ref.col_vec, 4),
        load(ref.inc_hbm, ref.inc, 5),
        load(ref.cost_hbm, ref.cost, 6),
        load(ref.start_hbm, ref.start, 7),
        load(ref.len_hbm, ref.len, 8),
        load(ref.cap_hbm.at[:, cap_lanes], ref.cap_in, 9),
    ]

    def load_blocks(chunk):
        span = pl.ds(chunk * GROUP, GROUP)
        return pltpu.make_async_copy(
            ref.values_hbm.at[span], ref.blocks.at[span], ref.block_sem.at[chunk]
        )

    for copy in loads[:5]:
        copy.start()
    for chunk in range(tiles // GROUP):
        load_blocks(chunk).start()
    for copy in loads[5:]:
        copy.start()

    me_z, me_y = me_r // 2, lax.rem(me_chip, 4)
    me_x = (me_chip // 4) * 2 + lax.rem(me_r, 2)
    along_x = [lax.rem(me_x + d, 4) for d in range(4)]
    row_z = [lax.rem(me_z + d, 4) * 2 for d in range(4)]
    row_x = [lax.rem(x, 2) for x in along_x]
    col_x = [(x // 2) * 8 for x in along_x]
    col_y = [lax.rem(me_y + d, 4) * 2 for d in range(4)]
    col_core = [me_core, 1 - me_core]

    def hops(offset):
        return sum(min(d, 4 - d) for d in offset[:-1]) + offset[-1] / 8

    def farthest_first(*sizes):
        return sorted(itertools.product(*map(range, sizes)), key=hops, reverse=True)[:-1]

    every_peer = [
        (row_z[dz] + row_x[dx], col_x[dx] + col_y[dy] + col_core[dc])
        for dz, dx, dy, dc in farthest_first(4, 4, 4, 2)
    ]
    row_peers = [
        (me_r, col_x[dx] + col_y[dy] + col_core[dc])
        for dx, dy, dc in sorted(
            ((2 * far, dy, dc) for far in range(2) for dy in range(4) for dc in range(2)),
            key=hops,
            reverse=True,
        )[:-1]
    ]

    barrier = pltpu.get_barrier_semaphore()

    for peer in every_peer:
        pl.semaphore_signal(barrier, inc=1, device_id=peer, device_id_type=MESH)

    def remote(source, target, send_sem, recv_sem, peer):
        return pltpu.make_async_remote_copy(
            src_ref=source,
            dst_ref=target,
            send_sem=send_sem,
            recv_sem=recv_sem,
            device_id=peer,
            device_id_type=MESH,
        )

    def place(buffer, r, c):
        return buffer.at[
            pl.ds(r * local_part, local_part),
            pl.ds(pl.multiple_of(c * block_rows, block_rows), block_rows),
        ]

    def slope_copy(part, peer):
        return remote(
            place(slope_send[part], *peer),
            slope_recv[part].at[me],
            ref.slope_send_sem.at[part],
            ref.slope_sem.at[part],
            peer,
        )

    def probe_copy(part, peer):
        return remote(
            probe_send[part].at[peer[1]],
            place(probe_recv[part], me_r, me_c),
            ref.probe_send_sem.at[part],
            ref.probe_sem.at[part],
            peer,
        )

    def all_blocks(part, send_sem, recv_sem):
        span = slope_recv[part].at[pl.ds(0, devices - 1)]
        return remote(span, span, send_sem.at[part], recv_sem.at[part], every_peer[0])

    def own_place(buffer, c):
        return buffer.at[
            pl.ds((c // 2) * local_part, local_part),
            pl.ds(pl.multiple_of(lax.rem(c, 2) * half_rows, half_rows), half_rows),
        ]

    def image_copy(part, index):
        return remote(
            own_place(image_send[part], row_peers[index][1]),
            image_recv[part].at[index],
            ref.image_send_sem.at[part],
            ref.image_sem.at[part],
            row_peers[index],
        )

    def dual_copy(part, index):
        return remote(
            own_place(duals_recv[part], me_c),
            own_place(duals_recv[part], me_c),
            ref.dual_send_sem.at[part],
            ref.dual_sem.at[part],
            row_peers[index],
        )

    def all_rows(part, send_sem, recv_sem):
        span = image_recv[part]
        return remote(span, span, send_sem.at[part], recv_sem.at[part], row_peers[0])

    def total(triangle, values):
        return jnp.dot(
            triangle, values, precision=lax.Precision.HIGHEST, preferred_element_type=F32
        )

    def pair(part, index_of, n, transposed):
        left = jnp.concatenate(
            [by_tile[part][index_of(n)], by_tile[part][index_of(n + 1)]], axis=0
        ).astype(BF16)
        if transposed:
            right = ref.blocks[pl.ds(n, 2)].reshape(256, 128)
            contract = (((1,), (1,)), ((), ()))
        else:
            right = jnp.concatenate([ref.blocks[n], ref.blocks[n + 1]], axis=1)
            contract = (((1,), (0,)), ((), ()))
        both = lax.dot_general(left, right, contract, preferred_element_type=F32)
        products[part][n] = both[:scen_part, :128]
        products[part][n + 1] = both[scen_part:, 128:]

    def row_index(n):
        return ref.row_of[0, n]

    def col_index(n):
        tile = ref.col_of[0, n]
        return lax.rem(tile, flight_tiles) * 8 + tile // flight_tiles

    def multiply(part, index_of, transposed):
        @pl.loop(0, tiles // UNROLLED)
        def _(group):
            for k in range(0, UNROLLED, 2):
                pair(part, index_of, group * UNROLLED + k, transposed)

    def multiply_arriving():
        @pl.loop(0, tiles // GROUP)
        def _(group):
            load_blocks(group).wait()
            for k in range(0, GROUP, 2):
                n = group * GROUP + k
                left = jnp.concatenate(
                    [by_tile[part][row_index(n + i)] for i in range(2) for part in parts], axis=0
                ).astype(BF16)
                right = jnp.concatenate([ref.blocks[n], ref.blocks[n + 1]], axis=1)
                both = jnp.dot(left, right, preferred_element_type=F32)
                for i in range(2):
                    for part in parts:
                        first = i * scenarios + part * scen_part
                        products[part][n + i] = both[
                            first : first + scen_part, i * 128 : (i + 1) * 128
                        ]

    def gathered(part, hot, position):
        both = jnp.concatenate(
            [flat[part][pl.ds(position + k, tiles, stride=scen_part), :] for k in range(2)], axis=1
        )
        high = both.astype(BF16)
        low = (both - high.astype(F32)).astype(BF16)
        return jnp.dot(
            hot[...], jnp.concatenate([high, low], axis=0), preferred_element_type=F32
        )

    def fold_slope(part, sweep):
        if sweep:
            all_blocks(part, ref.slope_send_sem, ref.slope_sem).wait_send()
        for position in range(0, scen_part, 2):
            summed = gathered(part, ref.hot_cols, position).astype(BF16)
            slope_send[part][position] = summed[:, :128]
            slope_send[part][position + 1] = summed[:, 128:]

    def send_slope(part):
        for peer in every_peer:
            slope_copy(part, peer).start()
        slope_recv[part][me] = place(slope_send[part], me_r, me_c)[...]

    def update_primal(part, sweep, upper, running, trailing):
        all_blocks(part, ref.slope_send_sem, ref.slope_sem).wait_recv()

        @pl.loop(0, n_col, unroll=4)
        def _(block):
            summed = slope_recv[part][block].astype(F32)
            for group in range(1, n_row):
                summed = summed + slope_recv[part][group * n_col + block].astype(F32)
            rows = pl.ds(pl.multiple_of(block * 8, 8), 8)
            for k in range(local_part):
                for half in range(flights // 128):
                    lanes = slice(half * 128, (half + 1) * 128)
                    ref.slope[k, rows, lanes] = (
                        summed[k, half * 8 : (half + 1) * 8] + ref.cost[rows, lanes]
                    )

        if sweep:
            all_blocks(part, ref.probe_send_sem, ref.probe_sem).wait_send()
        for k in range(local_part):
            scen = part * local_part + k
            before = ref.inc if sweep == 0 else ref.primal
            gradient = total(trailing, ref.slope[k])
            fresh = jnp.clip(before[scen] - tau_step * gradient, 0.0, upper)
            ref.primal[scen] = fresh
            fresh_sum = total(running, fresh)
            probe = 2.0 * fresh_sum - ref.cumulative[scen]
            ref.cumulative[scen] = fresh_sum
            for block in range(n_col):
                probe_send[part][block, k] = jnp.concatenate(
                    [
                        probe[block * 8 : (block + 1) * 8, half * 128 : (half + 1) * 128]
                        for half in range(flights // 128)
                    ],
                    axis=0,
                ).astype(BF16)

        for peer in every_peer:
            probe_copy(part, peer).start()

        place(probe_recv[part], me_r, me_c)[...] = probe_send[part][me_c]

    def send_image(part, sweep):
        all_blocks(part, ref.probe_send_sem, ref.probe_sem).wait_recv()
        for position in range(scen_part):
            by_row[part][pl.ds(position, col_tiles, stride=scen_part), :] = probe_recv[part][
                position
            ].astype(F32)
        multiply(part, col_index, True)
        if sweep:
            all_rows(part, ref.image_send_sem, ref.image_sem).wait_send()
        for position in range(0, scen_part, 2):
            summed = gathered(part, ref.hot_rows, position).astype(BF16)
            image_send[part][position] = summed[:, :128]
            image_send[part][position + 1] = summed[:, 128:]

        for index in range(n_col - 1):
            image_copy(part, index).start()

    def update_duals(part, sweep):
        all_rows(part, ref.image_send_sem, ref.image_sem).wait_recv()
        image = own_place(image_send[part], me_c)[...].astype(F32)
        for block in range(n_col - 1):
            image = image + image_recv[part][block].astype(F32)
        updated = jnp.maximum(
            ref.own_dual[part] + SIGMA_STEP * (image - ref.own_cap[part]), 0.0
        )
        ref.own_dual[part] = updated
        if sweep:
            all_rows(part, ref.dual_send_sem, ref.dual_sem).wait_send()
        own_place(duals_recv[part], me_c)[...] = updated.astype(BF16)

        for index in range(n_col - 1):
            dual_copy(part, index).start()

    def receive_duals(part):
        all_rows(part, ref.dual_send_sem, ref.dual_sem).wait_recv()

    loads[0].wait()

    @pl.loop(0, row_tiles // 8)
    def _(group):
        for k in range(8):
            tile = group * 8 + k
            ref.staged[pl.ds(pl.multiple_of(tile * scenarios, scenarios), scenarios), :] = (
                ref.dual_in[:, pl.ds(pl.multiple_of(tile * 128, 128), 128)]
            )

    for part in parts:
        by_row[part][0 : row_tiles * scen_part, :] = ref.staged[
            pl.ds(part, row_tiles * scen_part, stride=PARTS), :
        ]
        for k in range(local_part):
            first = me_core * half_rows * scenarios + scenario_of(part, me_chip * local_part + k)
            ref.own_dual[part, k] = ref.staged[pl.ds(first, half_rows, stride=scenarios), :]
    for copy in loads[1:5]:
        copy.wait()
    where_col = lax.rem(ref.col_vec[...], flight_tiles) * 8 + ref.col_vec[...] // flight_tiles
    hot = (where_col == lax.broadcasted_iota(jnp.int32, (col_tiles, tiles), 0)).astype(F32)
    ref.hot_cols[...] = jnp.concatenate([hot, hot], axis=1).astype(BF16)

    multiply_arriving()
    for part in parts:
        fold_slope(part, 0)
        if part == 0:
            pl.semaphore_wait(barrier, devices - 1)
        send_slope(part)

    hot = (
        ref.row_vec[...] == lax.broadcasted_iota(jnp.int32, (row_tiles, tiles), 0)
    ).astype(F32)
    ref.hot_rows[...] = jnp.concatenate([hot, hot], axis=1).astype(BF16)
    for copy in loads[5:]:
        copy.wait()

    @pl.loop(0, half_rows // 8)
    def _(group):
        for k in range(8):
            tile = group * 8 + k
            ref.staged[pl.ds(pl.multiple_of(tile * scenarios, scenarios), scenarios), :] = (
                ref.cap_in[:, pl.ds(pl.multiple_of(tile * 128, 128), 128)].astype(F32)
            )

    for part in parts:
        for k in range(local_part):
            first = scenario_of(part, me_chip * local_part + k)
            ref.own_cap[part, k] = ref.staged[pl.ds(first, half_rows, stride=scenarios), :]

    row_iota = lax.broadcasted_iota(jnp.int32, (window, window), 0)
    col_iota = lax.broadcasted_iota(jnp.int32, (window, window), 1)
    running = (row_iota >= col_iota).astype(F32)
    trailing = (row_iota <= col_iota).astype(F32)
    for scen in range(scen_local):
        ref.cumulative[scen] = total(running, ref.inc[scen])
    minutes = lax.broadcasted_iota(jnp.int32, (window, flights), 0)
    upper = (
        (minutes >= ref.start[...]) & (minutes < ref.start[...] + ref.len[...])
    ).astype(F32)

    for sweep in range(ITERS):
        for part in parts:
            update_primal(part, sweep, upper, running, trailing)
        for part in parts:
            send_image(part, sweep)
        for part in parts:
            update_duals(part, sweep)
        for part in parts:
            receive_duals(part)
            for position in range(scen_part):
                if sweep < ITERS - 1:
                    target, rows = by_row[part], pl.ds(position, row_tiles, stride=scen_part)
                else:
                    target = ref.staged
                    rows = pl.ds(scenario_of(part, position), row_tiles, stride=scenarios)
                target[rows, :] = duals_recv[part][position].astype(F32)
            if sweep < ITERS - 1:
                multiply(part, row_index, False)
                fold_slope(part, sweep + 1)
                send_slope(part)

    @pl.loop(0, row_tiles // 8)
    def _(group):
        for k in range(8):
            tile = group * 8 + k
            ref.duals[:, pl.ds(pl.multiple_of(tile * 128, 128), 128)] = ref.staged[
                pl.ds(pl.multiple_of(tile * scenarios, scenarios), scenarios), :
            ]

    for part in parts:
        all_blocks(part, ref.slope_send_sem, ref.slope_sem).wait_send()
        all_blocks(part, ref.probe_send_sem, ref.probe_sem).wait_send()
        all_rows(part, ref.image_send_sem, ref.image_sem).wait_send()
        all_rows(part, ref.dual_send_sem, ref.dual_sem).wait_send()


def per_device(
    tile_values,
    tile_rows,
    tile_cols,
    increments,
    dual_vars,
    flight_cost,
    win_start,
    win_len,
    capacity,
):
    n_row, n_col = lax.axis_size("row"), lax.axis_size("col")
    tiles, side = tile_values.shape[2], tile_values.shape[3]
    scen_local, window, flight_local = increments.shape
    scenarios, row_length = dual_vars.shape
    row_tiles = row_length // side
    time_block = window // n_col
    col_tiles = time_block * flight_local * n_col // side
    devices = n_row * n_col
    scen_part, local_part = scenarios // PARTS, scen_local // PARTS
    assert side == 128 and time_block == 8 and flight_local == 256
    assert scenarios == n_col and scen_local == 2
    dims = (n_row, n_col, scenarios, scen_local, window, tiles, row_tiles, col_tiles)
    vmem = pl.BlockSpec(memory_space=pltpu.VMEM)
    inputs = dict(
        values_hbm=tile_values.reshape(tiles, side, side),
        rows_hbm=tile_rows.reshape(1, tiles),
        cols_hbm=tile_cols.reshape(1, tiles),
        inc_hbm=increments,
        dual_hbm=dual_vars,
        cost_hbm=flight_cost,
        start_hbm=win_start.reshape(1, flight_local),
        len_hbm=win_len.reshape(1, flight_local),
        cap_hbm=capacity,
    )
    dma = pltpu.SemaphoreType.DMA
    scratch = dict(
        row_of=pltpu.SMEM((1, tiles), jnp.int32),
        col_of=pltpu.SMEM((1, tiles), jnp.int32),
        row_vec=pltpu.VMEM((1, tiles), jnp.int32),
        col_vec=pltpu.VMEM((1, tiles), jnp.int32),
        inc=pltpu.VMEM(increments.shape, F32),
        dual_in=pltpu.VMEM(dual_vars.shape, F32),
        cost=pltpu.VMEM(flight_cost.shape, F32),
        start=pltpu.VMEM((1, flight_local), jnp.int32),
        len=pltpu.VMEM((1, flight_local), jnp.int32),
        cap_in=pltpu.VMEM((scenarios, row_length // 2), jnp.int32),
        blocks=pltpu.VMEM((tiles, side, side), BF16),
        hot_cols=pltpu.VMEM((col_tiles, 2 * tiles), BF16),
        hot_rows=pltpu.VMEM((row_tiles, 2 * tiles), BF16),
        staged=pltpu.VMEM((row_tiles * scenarios, side), F32),
        slope=pltpu.VMEM((local_part, window, flight_local), F32),
        cumulative=pltpu.VMEM(increments.shape, F32),
        own_dual=pltpu.VMEM((PARTS, local_part, row_tiles // 2, side), F32),
        own_cap=pltpu.VMEM((PARTS, local_part, row_tiles // 2, side), F32),
        load_sem=dma((10,)),
        block_sem=dma((tiles // GROUP,)),
        slope_send_sem=dma((PARTS,)),
        slope_sem=dma((PARTS,)),
        probe_send_sem=dma((PARTS,)),
        probe_sem=dma((PARTS,)),
        image_send_sem=dma((PARTS,)),
        image_sem=dma((PARTS,)),
        dual_send_sem=dma((PARTS,)),
        dual_sem=dma((PARTS,)),
    )
    for part in range(PARTS):
        scratch.update(
            {
                f"by_tile{part}": pltpu.VMEM((max(col_tiles, row_tiles), scen_part, side), F32),
                f"products{part}": pltpu.VMEM((tiles, scen_part, side), F32),
                f"slope_send{part}": pltpu.VMEM((scen_part, col_tiles, side), BF16),
                f"slope_recv{part}": pltpu.VMEM((devices, local_part, 16, side), BF16),
                f"probe_send{part}": pltpu.VMEM((n_col, local_part, 16, side), BF16),
                f"probe_recv{part}": pltpu.VMEM((scen_part, col_tiles, side), BF16),
                f"image_send{part}": pltpu.VMEM((scen_part, row_tiles, side), BF16),
                f"image_recv{part}": pltpu.VMEM((n_col - 1, local_part, row_tiles // 2, side), BF16),
                f"duals_recv{part}": pltpu.VMEM((scen_part, row_tiles, side), BF16),
            }
        )
    names = tuple(inputs) + ("primal", "duals") + tuple(scratch)
    return pl.pallas_call(
        functools.partial(kernel, dims, names),
        out_shape=(
            jax.ShapeDtypeStruct(increments.shape, F32),
            jax.ShapeDtypeStruct(dual_vars.shape, F32),
        ),
        in_specs=[pl.BlockSpec(memory_space=pl.ANY)] * len(inputs),
        out_specs=(vmem, vmem),
        scratch_shapes=list(scratch.values()),
        compiler_params=pltpu.CompilerParams(
            collective_id=0, has_side_effects=True, vmem_limit_bytes=56 * 1024 * 1024
        ),
    )(*inputs.values())


def solution(mesh):
    placed = (
        P("row", "col", None, None, None),
        P("row", "col", None),
        P("row", "col", None),
        P("row", None, "col"),
        P(None, "row"),
        P(None, "col"),
        P("col"),
        P("col"),
        P(None, "row"),
    )
    return jax.shard_map(
        per_device,
        mesh=mesh,
        in_specs=placed,
        out_specs=(P("row", None, "col"), P(None, "row")),
        check_vma=False,
    )
```
